32 devices in a mesh: prompts: 2 (over y), patch: 4 (over z), cfg: 2 (over core), batch: 2 (over x).
Axes of the slice: x: 2, y: 2, z: 4, core: 2. Of those that a mesh axis runs over, the one named last changes fastest.
Arguments:
- latent: float32 [4, 64, 1280], P(('prompts', 'batch'), 'patch'), parts along dimension 0, may hold values from -16 to 16
- stale_keys: bfloat16 [4, 64, 1280], P('prompts', 'patch', 'batch'), parts along dimension 0, may hold values from -18 to 18
- stale_values: bfloat16 [4, 64, 1280], P('prompts', 'patch', 'batch'), parts along dimension 0, may hold values from -12 to 12
- text_keys: bfloat16 [4, 77, 1280], P(('prompts', 'cfg'), None, 'batch'), parts along dimension 0, may hold values from -160 to 160
- text_values: bfloat16 [4, 77, 1280], P(('prompts', 'cfg'), None, 'batch'), parts along dimension 0, may hold values from -6 to 6
- w_query: bfloat16 [1280, 1280], P(None, 'batch'), may hold values from -0.15625 to 0.15625
- w_key: bfloat16 [1280, 1280], P(None, 'batch'), may hold values from -0.15625 to 0.15625
- w_value: bfloat16 [1280, 1280], P(None, 'batch'), may hold values from -0.15625 to 0.15625
- w_out: bfloat16 [1280, 1280], P('batch'), may hold values from -0.15625 to 0.15625
- norm_gain: float32 [1280], replicated, may hold values from 0.25 to 1.75
- norm_bias: float32 [1280], replicated, may hold values from -0.5 to 0.5
- timesteps: int32 [6], P('prompts'), parts along dimension 0, may hold values from 0 to 999, as said below
Outputs:
- final_latent: float32 [4, 64, 1280], P(('prompts', 'batch'), 'patch'), parts along dimension 0
- final_keys: bfloat16 [4, 64, 1280], P('prompts', 'patch', 'batch'), parts along dimension 0
- final_values: bfloat16 [4, 64, 1280], P('prompts', 'patch', 'batch'), parts along dimension 0
The draws below stay inside these ranges and needn't reach their ends.
There are 2 independent parts, one for each index of `prompts`. The reference program is written for one: setup_inputs(seed, part) draws one part's arguments, and reference() takes and returns one part's arrays. A program takes and returns all parts, laid end to end along the dimension named above; an argument that names none is the same for every part. Nothing has to cross between parts.
Inputs may be any that keep to these rules, and one draw needn't show every extreme that they name: `timesteps`: strictly falling from the first entry to the last.
All inputs are finite; a program needn't handle non-finite values.
Results may differ from the reference program's by a relative error of at most 0.035.
Values may be sent and summed in bfloat16 or wider, within the bound.
No kernel may reach another device: no remote copies, remote signals or barrier semaphores. Data moves between devices by JAX's collectives and lax.ppermute only.
A program may use at most 64 MiB of HBM per device.

```python
import math
import jax
import jax.numpy as jnp
from jax import lax

D = 1280
HEADS = 20
HEAD = 64
GROUPS = 32
CTX = 77
STEPS = 2
TOK_DEV = 16
TOKENS = 64
IMAGES = 2
N_PATCH = 4


def draw_latent(key, part):
    base = jax.random.normal(key, (IMAGES, TOKENS, D), jnp.float32)
    place = jnp.arange(TOKENS, dtype=jnp.float32) / max(TOKENS - 1, 1)
    rising = 1.0 + 2.0 * place
    return jnp.clip(base * rising[None, :, None], -16.0, 16.0)


def draw_text_keys(key, part):
    base = jnp.clip(jax.random.normal(key, (2, CTX, D), jnp.float32), -4.0, 4.0)
    return base.astype(jnp.bfloat16)


def draw_timesteps(key, part):
    first = jax.random.randint(jax.random.fold_in(key, 1), (1,), 700, 1000)
    drops = jax.random.randint(jax.random.fold_in(key, 2), (STEPS,), 60, 301)
    falls = jnp.concatenate([jnp.zeros((1,), jnp.int32), jnp.cumsum(drops).astype(jnp.int32)])
    return (first.astype(jnp.int32) - falls).astype(jnp.int32)


def steps_of(own_key, dims, pieces, low, high):
    def one(position, blocks):
        steps = jax.random.uniform(jax.random.fold_in(jax.random.fold_in(own_key, 6), position), (blocks,), jnp.float32, low / len(pieces), high / len(pieces))
        return jnp.repeat(jnp.exp(steps), dims[position] // blocks).reshape((-1,) + (1,) * (len(dims) - position - 1))

    factor_of = one(*pieces[0])
    for cut in pieces[1:]:
        factor_of = factor_of * one(*cut)
    return factor_of


def gaussian(stream_key, extent, scale, reach, split=(), kind=jnp.bfloat16):
    factor_of = steps_of(stream_key, extent, split, -0.22, 0.18) if split else 1.0
    result = jax.random.normal(stream_key, extent, jnp.float32) * scale * factor_of
    return jnp.minimum(jnp.maximum(result, -reach), reach).astype(kind)


def setup_inputs(seed: int = 0, part: int = 0) -> dict:
    key_of = jax.random.split(jax.random.key(seed), 13)
    part_keys = jax.random.split(jax.random.fold_in(key_of[12], part), 13)
    return {
        "latent": draw_latent(jax.random.fold_in(jax.random.fold_in(key_of[12], part), 71), part),
        "stale_keys": gaussian(part_keys[1], (IMAGES, TOKENS, D), 3.0, 18.0, ((1, 4), (2, 2))),
        "stale_values": gaussian(part_keys[2], (IMAGES, TOKENS, D), 2.0, 12.0, ((1, 4), (2, 2))),
        "text_keys": draw_text_keys(jax.random.fold_in(jax.random.fold_in(key_of[12], part), 71), part),
        "text_values": gaussian(part_keys[4], (2, CTX, D), 1.0, 6.0, ((0, 2), (2, 2))),
        "w_query": gaussian(key_of[5], (D, D), D ** -0.5, 0.15625, ((1, 2),)),
        "w_key": gaussian(key_of[6], (D, D), D ** -0.5, 0.15625, ((1, 2),)),
        "w_value": gaussian(key_of[7], (D, D), D ** -0.5, 0.15625, ((1, 2),)),
        "w_out": gaussian(key_of[8], (D, D), D ** -0.5, 0.15625, ((0, 2),)),
        "norm_gain": jnp.clip(1.0 + 0.15 * jax.random.normal(key_of[9], (D,), jnp.float32), 0.25, 1.75),
        "norm_bias": jnp.clip(jax.random.uniform(key_of[10], (D,), jnp.float32, -0.5, 0.5), -0.5, 0.5),
        "timesteps": draw_timesteps(jax.random.fold_in(jax.random.fold_in(key_of[12], part), 71), part),
    }


guide_weight = 5.0
norm_eps = 1e-06

def alpha_bar(step_index):
    grid = jnp.arange(1000, dtype=jnp.int32)
    ramp = grid.astype(jnp.float32) / 999.0
    root = math.sqrt(0.00085) + ramp * (math.sqrt(0.012) - math.sqrt(0.00085))
    logs = jnp.cumsum(jnp.log1p(-root * root))
    picked = (grid == step_index).astype(jnp.float32)
    return jnp.exp(jnp.sum(picked * logs))

def sampler_weights(now, after):
    a_now = alpha_bar(now)
    a_next = alpha_bar(after)
    keep = jnp.sqrt(a_next / a_now)
    push = jnp.sqrt(1.0 - a_next) - keep * jnp.sqrt(1.0 - a_now)
    return (keep, push)

def group_norm(state, gain, bias):
    images, tokens, width = state.shape
    grouped = state.reshape(images, tokens, GROUPS, width // GROUPS)
    mean = lax.optimization_barrier(jnp.mean(grouped, axis=(1, 3), keepdims=True))
    square = lax.optimization_barrier(jnp.mean(grouped * grouped, axis=(1, 3), keepdims=True))
    scale = lax.rsqrt(square - mean * mean + norm_eps)
    normed = ((grouped - mean) * scale).reshape(images, tokens, width) * gain + bias
    return normed.astype(jnp.bfloat16)

def attend(queries, fresh_k, fresh_v, prior_k, prior_v, text_k, text_v):
    images, tokens, width = queries.shape
    text_kb = jnp.broadcast_to(text_k[None], (images,) + text_k.shape).astype(jnp.float32)
    text_vb = jnp.broadcast_to(text_v[None], (images,) + text_v.shape).astype(jnp.float32)

    def one_patch(patch):
        start = (patch * TOK_DEV).astype(jnp.int32)
        query = lax.dynamic_slice_in_dim(queries, start, TOK_DEV, 1).astype(jnp.float32)
        keys = lax.dynamic_update_slice_in_dim(prior_k, lax.dynamic_slice_in_dim(fresh_k, start, TOK_DEV, 1), start, 1)
        values = lax.dynamic_update_slice_in_dim(prior_v, lax.dynamic_slice_in_dim(fresh_v, start, TOK_DEV, 1), start, 1)
        keys = jnp.concatenate([keys.astype(jnp.float32), text_kb], axis=1)
        values = jnp.concatenate([values.astype(jnp.float32), text_vb], axis=1)
        query = query.reshape(images, TOK_DEV, HEADS, HEAD)
        keys = keys.reshape(images, keys.shape[1], HEADS, HEAD)
        values = values.reshape(images, values.shape[1], HEADS, HEAD)
        scores = jnp.einsum('bqhd,bkhd->bhqk', query, keys) * HEAD ** (-0.5)
        top = lax.optimization_barrier(jnp.max(scores, axis=-1, keepdims=True))
        weights = jnp.exp(scores - top)
        probs = (weights / lax.optimization_barrier(jnp.sum(weights, axis=-1, keepdims=True))).astype(jnp.bfloat16)
        out = jnp.einsum('bhqk,bkhd->bqhd', probs.astype(jnp.float32), values)
        return out.reshape(images, TOK_DEV, width).astype(jnp.bfloat16)
    blocks = lax.map(one_patch, jnp.arange(N_PATCH, dtype=jnp.int32))
    return jnp.transpose(blocks, (1, 0, 2, 3)).reshape(images, tokens, width)

def reference(latent, stale_keys, stale_values, text_keys, text_values, w_query, w_key, w_value, w_out, norm_gain, norm_bias, timesteps):
    state = latent
    images, tokens, width = latent.shape
    prior_k, prior_v = (stale_keys, stale_values)
    for step in range(STEPS):
        normed = group_norm(state, norm_gain, norm_bias)
        flat = normed.reshape(images * tokens, width)
        queries = jnp.dot(flat, w_query, preferred_element_type=jnp.float32).astype(jnp.bfloat16).reshape(images, tokens, width)
        fresh_k = jnp.dot(flat, w_key, preferred_element_type=jnp.float32).astype(jnp.bfloat16).reshape(images, tokens, width)
        fresh_v = jnp.dot(flat, w_value, preferred_element_type=jnp.float32).astype(jnp.bfloat16).reshape(images, tokens, width)
        branches = []
        for half in range(2):
            attended = attend(queries, fresh_k, fresh_v, prior_k, prior_v, text_keys[half], text_values[half])
            mixed = jnp.dot(attended.reshape(images * tokens, width), w_out, preferred_element_type=jnp.float32)
            branches.append(state + mixed.reshape(images, tokens, width))
        guess = branches[1] + guide_weight * (branches[0] - branches[1])
        keep, push = sampler_weights(timesteps[step], timesteps[step + 1])
        state = keep * state + push * guess
        prior_k, prior_v = (fresh_k, fresh_v)
    return (state, prior_k, prior_v)
```

```python
import functools
import math

import jax
import jax.numpy as jnp
from jax import lax
from jax.experimental import pallas as pl
from jax.experimental.pallas import tpu as pltpu
from jax.sharding import PartitionSpec as P

HEAD = 64
GROUPS = 32
STEPS = 2
LANES = 128
ROW_BLOCK = 64

guide_weight = 5.0
norm_eps = 1e-06


VMEM = pl.BlockSpec(memory_space=pltpu.VMEM)
SMEM = pl.BlockSpec(memory_space=pltpu.SMEM)


def sampler_kernel(steps, t_ref, out_ref):
    shape = (8, LANES)
    grid = lax.broadcasted_iota(jnp.int32, shape, 0) * LANES + lax.broadcasted_iota(
        jnp.int32, shape, 1
    )
    ramp = grid.astype(jnp.float32) / 999.0
    root = math.sqrt(0.00085) + ramp * (math.sqrt(0.012) - math.sqrt(0.00085))
    logs = jnp.log1p(-root * root)

    def alpha_bar(t):
        picked = jnp.where(grid <= t, logs, 0.0)
        return jnp.exp(jnp.sum(jnp.sum(picked, axis=1, keepdims=True), axis=0, keepdims=True))

    bars = [alpha_bar(t_ref[k]) for k in range(steps + 1)]
    for k in range(steps):
        keep = jnp.sqrt(bars[k + 1] / bars[k])
        push = jnp.sqrt(1.0 - bars[k + 1]) - keep * jnp.sqrt(1.0 - bars[k])
        out_ref[2 * k : 2 * k + 1, :] = jnp.broadcast_to(keep, (1, LANES))
        out_ref[2 * k + 1 : 2 * k + 2, :] = jnp.broadcast_to(push, (1, LANES))


def sampler_weights(timesteps):
    return pl.pallas_call(
        functools.partial(sampler_kernel, STEPS),
        out_shape=jax.ShapeDtypeStruct((2 * STEPS, LANES), jnp.float32),
        in_specs=[SMEM],
        out_specs=VMEM,
        name="sampler",
    )(timesteps)


def split3(x):
    hi = x.astype(jnp.bfloat16)
    rest = x - hi.astype(jnp.float32)
    mid = rest.astype(jnp.bfloat16)
    low = (rest - mid.astype(jnp.float32)).astype(jnp.bfloat16)
    return [hi.astype(jnp.float32), mid.astype(jnp.float32), low.astype(jnp.float32)]


def stack8(rows):
    pad = jnp.zeros((8 - len(rows),) + rows[0].shape[1:], jnp.float32)
    return jnp.concatenate(list(rows) + [pad], axis=0).astype(jnp.bfloat16)


def norm_factors(state, gain):
    rows, width = state.shape
    per = width // GROUPS
    sums = jnp.sum(state, axis=0, keepdims=True)
    squares = jnp.sum(state * state, axis=0, keepdims=True)
    channel = lax.broadcasted_iota(jnp.int32, (width, LANES), 0)
    first = lax.broadcasted_iota(jnp.int32, (width, LANES), 1) * per
    member = ((channel >= first) & (channel < first + per)).astype(jnp.float32).astype(jnp.bfloat16)
    parts = jnp.dot(
        stack8(split3(sums) + split3(squares)), member, preferred_element_type=jnp.float32
    )
    count = float(rows * per)
    mean = (parts[0:1] + parts[1:2] + parts[2:3]) / count
    square = (parts[3:4] + parts[4:5] + parts[5:6]) / count
    scale = lax.rsqrt(square - mean * mean + norm_eps)
    channel_t = lax.broadcasted_iota(jnp.int32, (LANES, width), 1)
    first_t = lax.broadcasted_iota(jnp.int32, (LANES, width), 0) * per
    member_t = ((channel_t >= first_t) & (channel_t < first_t + per)).astype(jnp.float32)
    lane = lax.broadcasted_iota(jnp.int32, (1, LANES), 1)
    scale = jnp.where(lane < GROUPS, scale, 0.0)
    wide = jnp.dot(
        stack8(split3(mean) + split3(scale)),
        member_t.astype(jnp.bfloat16),
        preferred_element_type=jnp.float32,
    )
    mean_c = wide[0:1] + wide[1:2] + wide[2:3]
    scale_c = wide[3:4] + wide[4:5] + wide[5:6]
    return mean_c, scale_c * gain


def dot_t(a, b):
    return lax.dot_general(a, b, (((1,), (1,)), ((), ())), preferred_element_type=jnp.float32)


def weigh(scores, allowed, values):
    if allowed is not None:
        scores = jnp.where(allowed, scores, -1e30)
    top = jnp.max(scores, axis=-1, keepdims=True)
    weights = jnp.exp(scores - top)
    total = jnp.sum(weights, axis=-1, keepdims=True)
    acc = jnp.dot(weights.astype(jnp.bfloat16), values, preferred_element_type=jnp.float32)
    return top, total, acc


def block_of(index, size):
    if size & (size - 1) == 0:
        return lax.shift_right_logical(index, size.bit_length() - 1)
    return index // size


def attend(q, keys, values, texts, ctx, guides, own_mask):
    rows, width = q.shape
    out = []
    for low in range(0, width, LANES):
        cut = slice(low, min(low + LANES, width))
        wide = cut.stop - cut.start
        heads = wide // HEAD
        qc = q[:, cut]
        lane = lax.broadcasted_iota(jnp.int32, (rows, wide), 1)
        picks = [(lane >= HEAD * h) & (lane < HEAD * (h + 1)) for h in range(heads)]
        stacked = jnp.concatenate([jnp.where(pick, qc, 0.0) for pick in picks], axis=0)
        stacked = stacked.astype(jnp.bfloat16)
        scores = dot_t(stacked, keys[:, cut])
        allowed = None
        if own_mask is not None:
            allowed = jnp.concatenate([own_mask] * heads, axis=0)
        top, total, acc = weigh(scores, allowed, values[:, cut])
        halves = []
        for tk, tv in texts:
            text_scores = dot_t(stacked, tk[:, cut])
            seen = lax.broadcasted_iota(jnp.int32, text_scores.shape, 1) < ctx
            halves.append(weigh(text_scores, seen, tv[:, cut]))
        near = 0.0
        mixed = 0.0
        for (t_top, t_total, t_acc), guide in zip(halves, guides):
            both = jnp.maximum(top, t_top)
            fade = jnp.exp(top - both)
            t_fade = jnp.exp(t_top - both)
            share = guide / (total * fade + t_total * t_fade)
            near = near + fade * share
            mixed = mixed + t_acc * (t_fade * share)
        mixed = mixed + acc * near
        piece = mixed[:rows]
        for h in range(1, heads):
            piece = jnp.where(picks[h], mixed[h * rows : (h + 1) * rows], piece)
        out.append(piece.astype(jnp.bfloat16))
    return out


def first_kernel(images, patches, ctx, refs):
    (guide_ref, samp, gain, bias, wq, wk, wv, wo, txt_a, txt_b, kv_own, lat_own) = refs[:12]
    n = 12
    lats = refs[n : n + images * (patches - 1)]
    n += images * (patches - 1)
    kvs = refs[n : n + patches - 1]
    n += patches - 1
    base, send, k_out, v_out = refs[n : n + 4]
    state_s, normed_s, q_s, key_s, val_s, att_s = refs[n + 4 :]
    tok = lat_own.shape[1]
    rows = tok * patches
    width = wq.shape[1]
    keep = samp[0:1, 0:1]
    push = samp[1:2, 0:1]
    guides = (guide_ref[0], guide_ref[1])
    texts = ((txt_a.at[0], txt_a.at[1]), (txt_b.at[0], txt_b.at[1]))
    for i in range(images):
        state_s[0:tok, :] = lat_own[i]
        for k in range(1, patches):
            state_s[k * tok : (k + 1) * tok, :] = lats[i * (patches - 1) + k - 1][...]
        mean, factor = norm_factors(state_s[...], gain[...])
        normed_s[...] = ((state_s[...] - mean) * factor + bias[...]).astype(jnp.bfloat16)
        normed = normed_s[...]
        q_s[...] = (
            jnp.dot(normed, wq[...], preferred_element_type=jnp.float32)
            .astype(jnp.bfloat16)
            .astype(jnp.float32)
            * HEAD ** (-0.5)
        )
        fresh = jnp.dot(normed, wk[...], preferred_element_type=jnp.float32).astype(jnp.bfloat16)
        key_s[rows : 2 * rows, :] = fresh
        k_out[i] = fresh
        fresh = jnp.dot(normed, wv[...], preferred_element_type=jnp.float32).astype(jnp.bfloat16)
        val_s[rows : 2 * rows, :] = fresh
        v_out[i] = fresh
        key_s[0:tok, :] = kv_own[0, i]
        val_s[0:tok, :] = kv_own[1, i]
        for k in range(1, patches):
            key_s[k * tok : (k + 1) * tok, :] = kvs[k - 1][0, i]
            val_s[k * tok : (k + 1) * tok, :] = kvs[k - 1][1, i]

        def block(start, size):
            row = lax.broadcasted_iota(jnp.int32, (size, 2 * rows), 0) + start
            col = lax.broadcasted_iota(jnp.int32, (size, 2 * rows), 1)
            fresh_col = col >= rows
            same = block_of(row, tok) == block_of(jnp.where(fresh_col, col - rows, col), tok)
            mask = same == fresh_col
            pieces = attend(
                q_s[pl.ds(start, size), :], key_s, val_s, texts, ctx, guides, mask
            )
            for n_piece, piece in enumerate(pieces):
                at = n_piece * LANES
                att_s[pl.ds(start, size), at : at + piece.shape[1]] = piece

        size = min(rows, ROW_BLOCK)
        if rows % size:
            size = tok
        if rows == size:
            block(0, rows)
        else:

            def step(j, carry):
                block(pl.multiple_of(j * size, size), size)
                return carry

            lax.fori_loop(0, rows // size, step, 0)
        part = push * jnp.dot(att_s[...], wo[...], preferred_element_type=jnp.float32)
        send[i] = part.astype(jnp.bfloat16)
        base[i] = (keep + push) * state_s[...] + part


def last_kernel(images, patches, ctx, peers, refs):
    (guide_ref, samp, gain, bias, wq, wk, wv, wo, txt_a, txt_b, base, k_old, v_old) = refs[:13]
    n = 13
    others = refs[n : n + peers]
    n += peers
    base_out, part_out, k_out, v_out = refs[n : n + 4]
    state_s, key_s, val_s = refs[n + 4 :]
    rows = state_s.shape[0]
    tok = rows // patches
    keep = samp[2:3, 0:1]
    push = samp[3:4, 0:1]
    guides = (guide_ref[0], guide_ref[1])
    texts = ((txt_a.at[0], txt_a.at[1]), (txt_b.at[0], txt_b.at[1]))
    for i in range(images):
        state = base[i]
        for other in others:
            state = state + other[i].astype(jnp.float32)
        state_s[...] = state
        mean, factor = norm_factors(state_s[...], gain[...])
        own = state_s[0:tok, :]
        normed = ((own - mean) * factor + bias[...]).astype(jnp.bfloat16)
        q = (
            jnp.dot(normed, wq[...], preferred_element_type=jnp.float32)
            .astype(jnp.bfloat16)
            .astype(jnp.float32)
            * HEAD ** (-0.5)
        )
        fresh = jnp.dot(normed, wk[...], preferred_element_type=jnp.float32).astype(jnp.bfloat16)
        key_s[0:tok, :] = fresh
        k_out[i] = fresh
        fresh = jnp.dot(normed, wv[...], preferred_element_type=jnp.float32).astype(jnp.bfloat16)
        val_s[0:tok, :] = fresh
        v_out[i] = fresh
        key_s[tok:rows, :] = k_old[i, tok:rows, :]
        val_s[tok:rows, :] = v_old[i, tok:rows, :]
        pieces = attend(q, key_s, val_s, texts, ctx, guides, None)
        att = jnp.concatenate(pieces, axis=1)
        part = push * jnp.dot(att, wo[...], preferred_element_type=jnp.float32)
        part_out[i] = part
        base_out[i] = (keep + push) * own + part


def kernel_call(body, name, args, outs, scratch):
    def run(*refs):
        body(refs)

    return pl.pallas_call(
        run,
        out_shape=[jax.ShapeDtypeStruct(s, d) for s, d in outs],
        in_specs=[SMEM] + [VMEM] * (len(args) - 1),
        out_specs=[VMEM] * len(outs),
        scratch_shapes=[pltpu.VMEM(s, d) for s, d in scratch],
        compiler_params=pltpu.CompilerParams(vmem_limit_bytes=56 * 2**20),
        name=name,
    )(*args)


class Grid:
    def __init__(self, mesh):
        self.axes = ("patch", "cfg", "batch")
        self.sizes = tuple(mesh.shape[a] for a in self.axes)

    def flat(self, p, c, b):
        return (p * self.sizes[1] + c) * self.sizes[2] + b

    def pull(self, x, source):
        pairs = []
        for p in range(self.sizes[0]):
            for c in range(self.sizes[1]):
                for b in range(self.sizes[2]):
                    src = source(p, c, b)
                    if src is not None and src != (p, c, b):
                        pairs.append((self.flat(*src), self.flat(p, c, b)))
        return lax.ppermute(x, self.axes, pairs)


def pick(stack, index):
    if len(stack) == 1:
        return stack[0]
    return lax.dynamic_index_in_dim(jnp.stack(stack), index, 0, keepdims=False)


def body(
    grid,
    latent,
    stale_keys,
    stale_values,
    text_keys,
    text_values,
    w_query,
    w_key,
    w_value,
    w_out,
    norm_gain,
    norm_bias,
    timesteps,
):
    patches, halves, batch = grid.sizes
    state = latent[0]
    tok, width = state.shape
    images = stale_keys.shape[0]
    mine = images // halves
    local = w_query.shape[1]
    ctx = text_keys.shape[1]
    ctx_pad = -(-ctx // 16) * 16
    rows = tok * patches
    c = lax.axis_index("cfg")
    b = lax.axis_index("batch")
    keeper = b // mine == c

    def latent_source(k, s):
        def source(p, cc, bb):
            x = cc * mine + (bb + k) % mine
            return ((p - s) % patches, cc if bb // mine == cc else 1 - cc, x)

        return source

    slots = [[None] * patches for _ in range(mine)]
    for s in reversed(range(patches)):
        for k in range(mine):
            slots[k][s] = grid.pull(state, latent_source(k, s))
    slots[0][0] = jnp.where(keeper, state, slots[0][0])
    lat = [
        [pick([slots[k][s] for k in range(mine)], (i - b) % mine) for s in range(patches)]
        for i in range(mine)
    ]
    kv_own = jnp.stack(
        [lax.dynamic_slice_in_dim(x, c * mine, mine, 0) for x in (stale_keys, stale_values)]
    )
    kvs = [
        grid.pull(kv_own, lambda p, cc, bb, s=s: ((p - s) % patches, cc, bb))
        for s in range(1, patches)
    ]
    txt_own = jnp.pad(
        jnp.concatenate([text_keys, text_values], axis=0), ((0, 0), (0, ctx_pad - ctx), (0, 0))
    )
    txt_other = grid.pull(txt_own, lambda p, cc, bb: (p, 1 - cc, bb))

    samp = sampler_weights(timesteps)
    first = c == 0
    guides = jnp.stack(
        [
            jnp.where(first, guide_weight, 1.0 - guide_weight),
            jnp.where(first, 1.0 - guide_weight, guide_weight),
        ]
    ).astype(jnp.float32)
    gain = norm_gain[None]
    bias = norm_bias[None]
    common = [guides, samp, gain, bias, w_query, w_key, w_value, w_out, txt_own, txt_other]

    base, send, k0, v0 = kernel_call(
        functools.partial(first_kernel, mine, patches, ctx),
        "first",
        common
        + [kv_own, jnp.stack([lat[i][0] for i in range(mine)])]
        + [lat[i][s] for i in range(mine) for s in range(1, patches)]
        + kvs,
        [
            ((mine, rows, width), jnp.float32),
            ((mine, rows, width), jnp.bfloat16),
            ((mine, rows, local), jnp.bfloat16),
            ((mine, rows, local), jnp.bfloat16),
        ],
        [
            ((rows, width), jnp.float32),
            ((rows, width), jnp.bfloat16),
            ((rows, local), jnp.float32),
            ((2 * rows, local), jnp.bfloat16),
            ((2 * rows, local), jnp.bfloat16),
            ((rows, local), jnp.bfloat16),
        ],
    )
    others = [
        grid.pull(send, lambda p, cc, bb, r=r: (p, cc, (bb + r) % batch)) for r in range(1, batch)
    ]
    base1, part1, k1, v1 = kernel_call(
        functools.partial(last_kernel, mine, patches, ctx, batch - 1),
        "last",
        common + [base, k0, v0] + others,
        [
            ((mine, tok, width), jnp.float32),
            ((mine, tok, width), jnp.float32),
            ((mine, tok, local), jnp.bfloat16),
            ((mine, tok, local), jnp.bfloat16),
        ],
        [
            ((rows, width), jnp.float32),
            ((rows, local), jnp.bfloat16),
            ((rows, local), jnp.bfloat16),
        ],
    )

    def part_for(target):
        return pick([part1[i] for i in range(mine)], target % mine)

    own_base = pick([base1[i] for i in range(mine)], b % mine)
    total = None
    for r in [mine] + [r for r in range(1, batch) if r != mine]:
        part = part_for((b - r) % batch)

        def to_keeper(p, cc, bb, r=r):
            if bb // mine == cc:
                return (p, cc, (bb + r) % batch)
            return (p, 1 - cc, bb) if r == mine else None

        def to_partner(p, cc, bb, r=r):
            return None if bb // mine == cc else (p, 1 - cc, (bb + r) % batch)

        ring = grid.pull(jnp.where(keeper, own_base, part) if r == mine else part, to_keeper)
        diag = grid.pull(part, to_partner)
        if r == mine:
            total = ring + jnp.where(keeper, own_base, diag)
        else:
            total = total + jnp.where(keeper, ring, diag)
    kv1 = jnp.stack([k1, v1])
    kv_far = grid.pull(kv1, lambda p, cc, bb: (p, 1 - cc, bb))
    low = jnp.where(first, kv1, kv_far)
    high = jnp.where(first, kv_far, kv1)
    both = jnp.concatenate([low, high], axis=1)
    return total[None], both[0], both[1]


def solution(mesh):
    return jax.shard_map(
        functools.partial(body, Grid(mesh)),
        mesh=mesh,
        in_specs=(
            P(("prompts", "batch"), "patch", None),
            P("prompts", "patch", "batch"),
            P("prompts", "patch", "batch"),
            P(("prompts", "cfg"), None, "batch"),
            P(("prompts", "cfg"), None, "batch"),
            P(None, "batch"),
            P(None, "batch"),
            P(None, "batch"),
            P("batch", None),
            P(),
            P(),
            P("prompts"),
        ),
        out_specs=(
            P(("prompts", "batch"), "patch", None),
            P("prompts", "patch", "batch"),
            P("prompts", "patch", "batch"),
        ),
        check_vma=False,
    )
```

```python
import functools
import math

import jax
import jax.numpy as jnp
from jax import lax
from jax.experimental import pallas as pl
from jax.experimental.pallas import tpu as pltpu
from jax.sharding import PartitionSpec as P

HEAD = 64
GROUPS = 32
STEPS = 2
LANES = 128
ROW_BLOCK = 64

guide_weight = 5.0
norm_eps = 1e-06


VMEM = pl.BlockSpec(memory_space=pltpu.VMEM)
SMEM = pl.BlockSpec(memory_space=pltpu.SMEM)
ANY = pl.BlockSpec(memory_space=pl.ANY)


def near(x):
    return pltpu.with_memory_space_constraint(x, pltpu.VMEM)


def stay(x):
    return pltpu.with_memory_space_constraint(x, pltpu.HBM)


def alpha_bars(t_ref):
    shape = (8, LANES)
    grid = lax.broadcasted_iota(jnp.int32, shape, 0) * LANES + lax.broadcasted_iota(
        jnp.int32, shape, 1
    )
    ramp = grid.astype(jnp.float32) / 999.0
    root = math.sqrt(0.00085) + ramp * (math.sqrt(0.012) - math.sqrt(0.00085))
    logs = jnp.log1p(-root * root)

    def alpha_bar(t):
        picked = jnp.where(grid <= t, logs, 0.0)
        return jnp.exp(jnp.sum(jnp.sum(picked, axis=1, keepdims=True), axis=0, keepdims=True))

    return [alpha_bar(t_ref[k]) for k in range(STEPS + 1)]


def sampler_weights(bars, k):
    keep = jnp.sqrt(bars[k + 1] / bars[k])
    push = jnp.sqrt(1.0 - bars[k + 1]) - keep * jnp.sqrt(1.0 - bars[k])
    return keep, push


def split3(x):
    hi = x.astype(jnp.bfloat16)
    rest = x - hi.astype(jnp.float32)
    mid = rest.astype(jnp.bfloat16)
    low = (rest - mid.astype(jnp.float32)).astype(jnp.bfloat16)
    return [hi.astype(jnp.float32), mid.astype(jnp.float32), low.astype(jnp.float32)]


def stack8(rows):
    pad = jnp.zeros((8 - len(rows),) + rows[0].shape[1:], jnp.float32)
    return jnp.concatenate(list(rows) + [pad], axis=0).astype(jnp.bfloat16)


def norm_factors(state, gain):
    rows, width = state.shape
    per = width // GROUPS
    sums = jnp.sum(state, axis=0, keepdims=True)
    squares = jnp.sum(state * state, axis=0, keepdims=True)
    channel = lax.broadcasted_iota(jnp.int32, (width, LANES), 0)
    first = lax.broadcasted_iota(jnp.int32, (width, LANES), 1) * per
    member = ((channel >= first) & (channel < first + per)).astype(jnp.float32).astype(jnp.bfloat16)
    parts = jnp.dot(
        stack8(split3(sums) + split3(squares)), member, preferred_element_type=jnp.float32
    )
    count = float(rows * per)
    mean = (parts[0:1] + parts[1:2] + parts[2:3]) / count
    square = (parts[3:4] + parts[4:5] + parts[5:6]) / count
    scale = lax.rsqrt(square - mean * mean + norm_eps)
    channel_t = lax.broadcasted_iota(jnp.int32, (LANES, width), 1)
    first_t = lax.broadcasted_iota(jnp.int32, (LANES, width), 0) * per
    member_t = ((channel_t >= first_t) & (channel_t < first_t + per)).astype(jnp.float32)
    lane = lax.broadcasted_iota(jnp.int32, (1, LANES), 1)
    scale = jnp.where(lane < GROUPS, scale, 0.0)
    wide = jnp.dot(
        stack8(split3(mean) + split3(scale)),
        member_t.astype(jnp.bfloat16),
        preferred_element_type=jnp.float32,
    )
    mean_c = wide[0:1] + wide[1:2] + wide[2:3]
    scale_c = wide[3:4] + wide[4:5] + wide[5:6]
    return mean_c, scale_c * gain


def dot_t(a, b):
    return lax.dot_general(a, b, (((1,), (1,)), ((), ())), preferred_element_type=jnp.float32)


def weigh(scores, allowed, values):
    if allowed is not None:
        scores = jnp.where(allowed, scores, -1e30)
    top = jnp.max(scores, axis=-1, keepdims=True)
    weights = jnp.exp(scores - top)
    total = jnp.sum(weights, axis=-1, keepdims=True)
    acc = jnp.dot(weights.astype(jnp.bfloat16), values, preferred_element_type=jnp.float32)
    return top, total, acc


def block_of(index, size):
    if size & (size - 1) == 0:
        return lax.shift_right_logical(index, size.bit_length() - 1)
    return index // size


def attend(q, keys, values, texts, ctx, guides, own_mask):
    rows, width = q.shape
    out = []
    for low in range(0, width, LANES):
        cut = slice(low, min(low + LANES, width))
        wide = cut.stop - cut.start
        heads = wide // HEAD
        qc = q[:, cut]
        lane = lax.broadcasted_iota(jnp.int32, (rows, wide), 1)
        picks = [(lane >= HEAD * h) & (lane < HEAD * (h + 1)) for h in range(heads)]
        stacked = jnp.concatenate([jnp.where(pick, qc, 0.0) for pick in picks], axis=0)
        stacked = stacked.astype(jnp.bfloat16)
        scores = dot_t(stacked, keys[:, cut])
        allowed = None
        if own_mask is not None:
            allowed = jnp.concatenate([own_mask] * heads, axis=0)
        top, total, acc = weigh(scores, allowed, values[:, cut])
        halves = []
        for tk, tv in texts:
            text_scores = dot_t(stacked, tk[:, cut])
            seen = lax.broadcasted_iota(jnp.int32, text_scores.shape, 1) < ctx
            halves.append(weigh(text_scores, seen, tv[:, cut]))
        near = 0.0
        mixed = 0.0
        for (t_top, t_total, t_acc), guide in zip(halves, guides):
            both = jnp.maximum(top, t_top)
            fade = jnp.exp(top - both)
            t_fade = jnp.exp(t_top - both)
            share = guide / (total * fade + t_total * t_fade)
            near = near + fade * share
            mixed = mixed + t_acc * (t_fade * share)
        mixed = mixed + acc * near
        piece = mixed[:rows]
        for h in range(1, heads):
            piece = jnp.where(picks[h], mixed[h * rows : (h + 1) * rows], piece)
        out.append(piece.astype(jnp.bfloat16))
    return out


def prepare_kernel(images, refs):
    keys, values, text_k, text_v, kv_out, txt_out = refs
    c = lax.axis_index("cfg")
    for i in range(images):
        kv_out[0, i] = keys[c * images + i]
        kv_out[1, i] = values[c * images + i]
    ctx, width = text_k.shape[1:]
    pad = jnp.zeros((txt_out.shape[1] - ctx, width), jnp.float32)
    for n, ref in enumerate((text_k, text_v)):
        rows = jnp.concatenate([ref[0].astype(jnp.float32), pad], axis=0)
        txt_out[n] = rows.astype(jnp.bfloat16)


def fetch(sources, targets, sems):
    copies = [
        pltpu.make_async_copy(src, dst, sems.at[n])
        for n, (src, dst) in enumerate(zip(sources, targets))
    ]
    for copy in copies:
        copy.start()
    return copies


def guidance():
    first = lax.axis_index("cfg") == 0
    return (
        jnp.where(first, guide_weight, 1.0 - guide_weight),
        jnp.where(first, 1.0 - guide_weight, guide_weight),
    )


def is_keeper(images):
    mine = lax.axis_index("batch") // images if images > 1 else lax.axis_index("batch")
    return mine == lax.axis_index("cfg")


def first_kernel(images, patches, ctx, refs):
    (t_ref, *weights, gain, bias, txt_a, txt_b, kv_own, lat_here) = refs[:11]
    n = 11
    lats = refs[n : n + images * patches]
    n += images * patches
    kvs = refs[n : n + patches - 1]
    n += patches - 1
    base, send, k_out, v_out, samp = refs[n : n + 5]
    wq, wk, wv, wo, sems, state_s, normed_s, q_s, key_s, val_s, att_s = refs[n + 5 :]
    copies = fetch(weights, (wq, wk, wv, wo), sems)
    tok = lat_here.shape[1]
    rows = tok * patches
    bars = alpha_bars(t_ref)
    for k in range(STEPS):
        for n_row, value in enumerate(sampler_weights(bars, k)):
            at = 2 * k + n_row
            samp[at : at + 1, :] = jnp.broadcast_to(value, (1, LANES))
    keep, push = sampler_weights(bars, 0)
    keeper = is_keeper(images)
    guides = guidance()
    texts = ((txt_a.at[0], txt_a.at[1]), (txt_b.at[0], txt_b.at[1]))
    for i in range(images):
        own = lats[i * patches][...]
        if images == 1:
            own = jnp.where(keeper, lat_here[0], own)
        state_s[0:tok, :] = own
        for k in range(1, patches):
            state_s[k * tok : (k + 1) * tok, :] = lats[i * patches + k][...]
        mean, factor = norm_factors(state_s[...], gain[...].reshape(1, -1))
        normed_s[...] = ((state_s[...] - mean) * factor + bias[...].reshape(1, -1)).astype(
            jnp.bfloat16
        )
        normed = normed_s[...]
        if i == 0:
            copies[0].wait()
        q_s[...] = (
            jnp.dot(normed, wq[...], preferred_element_type=jnp.float32)
            .astype(jnp.bfloat16)
            .astype(jnp.float32)
            * HEAD ** (-0.5)
        )
        if i == 0:
            copies[1].wait()
        fresh = jnp.dot(normed, wk[...], preferred_element_type=jnp.float32).astype(jnp.bfloat16)
        key_s[rows : 2 * rows, :] = fresh
        k_out[i] = fresh
        if i == 0:
            copies[2].wait()
        fresh = jnp.dot(normed, wv[...], preferred_element_type=jnp.float32).astype(jnp.bfloat16)
        val_s[rows : 2 * rows, :] = fresh
        v_out[i] = fresh
        key_s[0:tok, :] = kv_own[0, i]
        val_s[0:tok, :] = kv_own[1, i]
        for k in range(1, patches):
            key_s[k * tok : (k + 1) * tok, :] = kvs[k - 1][0, i]
            val_s[k * tok : (k + 1) * tok, :] = kvs[k - 1][1, i]

        def block(start, size):
            row = lax.broadcasted_iota(jnp.int32, (size, 2 * rows), 0) + start
            col = lax.broadcasted_iota(jnp.int32, (size, 2 * rows), 1)
            fresh_col = col >= rows
            same = block_of(row, tok) == block_of(jnp.where(fresh_col, col - rows, col), tok)
            mask = same == fresh_col
            pieces = attend(
                q_s[pl.ds(start, size), :], key_s, val_s, texts, ctx, guides, mask
            )
            for n_piece, piece in enumerate(pieces):
                at = n_piece * LANES
                att_s[pl.ds(start, size), at : at + piece.shape[1]] = piece

        size = min(rows, ROW_BLOCK)
        if rows % size:
            size = tok
        if rows == size:
            block(0, rows)
        else:

            def step(j, carry):
                block(pl.multiple_of(j * size, size), size)
                return carry

            lax.fori_loop(0, rows // size, step, 0)
        if i == 0:
            copies[3].wait()
        part = push * jnp.dot(att_s[...], wo[...], preferred_element_type=jnp.float32)
        send[i] = part.astype(jnp.bfloat16)
        base[i] = (keep + push) * state_s[...] + part


def last_kernel(images, patches, ctx, peers, refs):
    (*weights, samp, gain, bias, txt_a, txt_b, base, k_old, v_old) = refs[:12]
    n = 12
    others = refs[n : n + peers]
    n += peers
    base_out, part_out, ring_out, kv_out = refs[n : n + 4]
    wq, wk, wv, wo, sems, state_s, key_s, val_s = refs[n + 4 :]
    copies = fetch(weights, (wq, wk, wv, wo), sems)
    rows = state_s.shape[0]
    tok = rows // patches
    keep = samp[2:3, 0:1]
    push = samp[3:4, 0:1]
    guides = guidance()
    texts = ((txt_a.at[0], txt_a.at[1]), (txt_b.at[0], txt_b.at[1]))
    for i in range(images):
        state = base[i]
        for other in others:
            state = state + other[i].astype(jnp.float32)
        state_s[...] = state
        mean, factor = norm_factors(state_s[...], gain[...].reshape(1, -1))
        own = state_s[0:tok, :]
        normed = ((own - mean) * factor + bias[...].reshape(1, -1)).astype(jnp.bfloat16)
        if i == 0:
            copies[0].wait()
        q = (
            jnp.dot(normed, wq[...], preferred_element_type=jnp.float32)
            .astype(jnp.bfloat16)
            .astype(jnp.float32)
            * HEAD ** (-0.5)
        )
        if i == 0:
            copies[1].wait()
        fresh = jnp.dot(normed, wk[...], preferred_element_type=jnp.float32).astype(jnp.bfloat16)
        key_s[0:tok, :] = fresh
        kv_out[0, i] = fresh
        if i == 0:
            copies[2].wait()
        fresh = jnp.dot(normed, wv[...], preferred_element_type=jnp.float32).astype(jnp.bfloat16)
        val_s[0:tok, :] = fresh
        kv_out[1, i] = fresh
        key_s[tok:rows, :] = k_old[i, tok:rows, :]
        val_s[tok:rows, :] = v_old[i, tok:rows, :]
        pieces = attend(q, key_s, val_s, texts, ctx, guides, None)
        att = jnp.concatenate(pieces, axis=1)
        if i == 0:
            copies[3].wait()
        part = push * jnp.dot(att, wo[...], preferred_element_type=jnp.float32)
        part_out[i] = part
        kept = (keep + push) * own + part
        base_out[i] = kept
        ring_out[i] = jnp.where(is_keeper(images), kept, part)


def end_kernel(images, extra, refs):
    base, ring, diag, kv, kv_far = refs[:5]
    others = refs[5 : 5 + 2 * extra]
    latent, keys, values = refs[5 + 2 * extra :]
    keeper = is_keeper(images)
    total = ring[...] + jnp.where(keeper, base[...], diag[...])
    for r in range(extra):
        total = total + jnp.where(keeper, others[2 * r][...], others[2 * r + 1][...])
    latent[0] = total
    c = lax.axis_index("cfg")
    for i in range(images):
        keys[c * images + i] = kv[0, i]
        values[c * images + i] = kv[1, i]
        keys[(1 - c) * images + i] = kv_far[0, i]
        values[(1 - c) * images + i] = kv_far[1, i]


def kernel_call(body, name, args, outs, scratch, scalars=0, weights=0, final=False):
    def run(*refs):
        body(refs)

    far = scalars + weights
    return pl.pallas_call(
        run,
        out_shape=[
            jax.ShapeDtypeStruct(s, d) if final else pltpu.VMEM(s, d) for s, d in outs
        ],
        in_specs=[SMEM] * scalars + [ANY] * weights + [VMEM] * (len(args) - far),
        out_specs=[VMEM] * len(outs),
        scratch_shapes=[pltpu.VMEM(w.shape, w.dtype) for w in args[scalars:far]]
        + ([pltpu.SemaphoreType.DMA((weights,))] if weights else [])
        + [pltpu.VMEM(s, d) for s, d in scratch],
        compiler_params=pltpu.CompilerParams(vmem_limit_bytes=32 * 2**20),
        name=name,
    )(*args)


class Grid:
    def __init__(self, mesh):
        self.axes = ("patch", "cfg", "batch")
        self.sizes = tuple(mesh.shape[a] for a in self.axes)

    def flat(self, p, c, b):
        return (p * self.sizes[1] + c) * self.sizes[2] + b

    def pull(self, x, source):
        pairs = []
        for p in range(self.sizes[0]):
            for c in range(self.sizes[1]):
                for b in range(self.sizes[2]):
                    src = source(p, c, b)
                    if src is not None and src != (p, c, b):
                        pairs.append((self.flat(*src), self.flat(p, c, b)))
        return lax.ppermute(x, self.axes, pairs)


def pick(stack, index):
    if len(stack) == 1:
        return stack[0]
    return lax.dynamic_index_in_dim(jnp.stack(stack), index, 0, keepdims=False)


def body(
    grid,
    latent,
    stale_keys,
    stale_values,
    text_keys,
    text_values,
    w_query,
    w_key,
    w_value,
    w_out,
    norm_gain,
    norm_bias,
    timesteps,
):
    patches, halves, batch = grid.sizes
    state = latent[0]
    tok, width = state.shape
    images = stale_keys.shape[0]
    mine = images // halves
    local = w_query.shape[1]
    ctx = text_keys.shape[1]
    ctx_pad = -(-ctx // 16) * 16
    rows = tok * patches
    b = lax.axis_index("batch")

    def away(p, s):
        return p ^ s if patches & (patches - 1) == 0 else (p - s) % patches

    def other_core(p, cc, bb):
        return (p, 1 - cc, bb)

    def latent_source(k, s):
        def source(p, cc, bb):
            if mine == 1 and s == 0:
                return (p, 1 - cc, 1 - bb)
            x = cc * mine + (bb + k) % mine
            return (away(p, s), cc if bb // mine == cc else 1 - cc, x)

        return source

    slots = [[grid.pull(state, latent_source(k, s)) for s in range(patches)] for k in range(mine)]
    if mine > 1:
        slots[0][0] = jnp.where(is_keeper(mine), state, slots[0][0])
    lat = [
        pick([slots[k][s] for k in range(mine)], (i - b) % mine)
        for i in range(mine)
        for s in range(patches)
    ]
    kv_own, txt_own = kernel_call(
        functools.partial(prepare_kernel, mine),
        "prepare",
        [stay(x) for x in (stale_keys, stale_values, text_keys, text_values)],
        [((2, mine, tok, local), jnp.bfloat16), ((2, ctx_pad, local), jnp.bfloat16)],
        [],
    )
    kvs = [
        grid.pull(kv_own, lambda p, cc, bb, s=s: (away(p, s), cc, bb)) for s in range(1, patches)
    ]
    txt_far = grid.pull(txt_own, other_core)

    weights = [stay(w) for w in (w_query, w_key, w_value, w_out)]
    affine = [stay(norm_gain), stay(norm_bias)]
    texts = [near(txt_own), near(txt_far)]
    base, send, k0, v0, samp = kernel_call(
        functools.partial(first_kernel, mine, patches, ctx),
        "first",
        [stay(timesteps)]
        + weights
        + affine
        + texts
        + [near(kv_own), stay(latent)]
        + [near(x) for x in lat + kvs],
        [
            ((mine, rows, width), jnp.float32),
            ((mine, rows, width), jnp.bfloat16),
            ((mine, rows, local), jnp.bfloat16),
            ((mine, rows, local), jnp.bfloat16),
            ((2 * STEPS, LANES), jnp.float32),
        ],
        [
            ((rows, width), jnp.float32),
            ((rows, width), jnp.bfloat16),
            ((rows, local), jnp.float32),
            ((2 * rows, local), jnp.bfloat16),
            ((2 * rows, local), jnp.bfloat16),
            ((rows, local), jnp.bfloat16),
        ],
        scalars=1,
        weights=len(weights),
    )
    others = [
        grid.pull(send, lambda p, cc, bb, r=r: (p, cc, (bb + r) % batch)) for r in range(1, batch)
    ]
    base1, part1, ring1, kv1 = kernel_call(
        functools.partial(last_kernel, mine, patches, ctx, batch - 1),
        "last",
        weights
        + [near(samp)]
        + affine
        + texts
        + [near(x) for x in [base, k0, v0] + others],
        [
            ((mine, tok, width), jnp.float32),
            ((mine, tok, width), jnp.float32),
            ((mine, tok, width), jnp.float32),
            ((2, mine, tok, local), jnp.bfloat16),
        ],
        [
            ((rows, width), jnp.float32),
            ((rows, local), jnp.bfloat16),
            ((rows, local), jnp.bfloat16),
        ],
        weights=len(weights),
    )

    kv_far = grid.pull(kv1, other_core)
    own_base = pick([base1[i] for i in range(mine)], b % mine)
    ends = []
    for r in [mine] + [r for r in range(1, batch) if r != mine]:
        part = pick([part1[i] for i in range(mine)], ((b - r) % batch) % mine)

        def to_keeper(p, cc, bb, r=r):
            if bb // mine == cc:
                return (p, cc, (bb + r) % batch)
            return (p, 1 - cc, bb) if r == mine else None

        def to_partner(p, cc, bb, r=r):
            if mine == 1:
                return (p, 1 - cc, 1 - bb)
            return None if bb // mine == cc else (p, 1 - cc, (bb + r) % batch)

        sent = part
        if r == mine:
            sent = ring1[0] if mine == 1 else jnp.where(is_keeper(mine), own_base, part)
        ends.append(grid.pull(sent, to_keeper))
        ends.append(grid.pull(part, to_partner))
    final = kernel_call(
        functools.partial(end_kernel, mine, batch - 2),
        "end",
        [near(x) for x in [own_base, ends[0], ends[1], kv1, kv_far] + ends[2:]],
        [
            ((1, tok, width), jnp.float32),
            ((images, tok, local), jnp.bfloat16),
            ((images, tok, local), jnp.bfloat16),
        ],
        [],
        final=True,
    )
    return tuple(final)


def solution(mesh):
    return jax.shard_map(
        functools.partial(body, Grid(mesh)),
        mesh=mesh,
        in_specs=(
            P(("prompts", "batch"), "patch", None),
            P("prompts", "patch", "batch"),
            P("prompts", "patch", "batch"),
            P(("prompts", "cfg"), None, "batch"),
            P(("prompts", "cfg"), None, "batch"),
            P(None, "batch"),
            P(None, "batch"),
            P(None, "batch"),
            P("batch", None),
            P(),
            P(),
            P("prompts"),
        ),
        out_specs=(
            P(("prompts", "batch"), "patch", None),
            P("prompts", "patch", "batch"),
            P("prompts", "patch", "batch"),
        ),
        check_vma=False,
    )
```

```python
import functools
import math

import jax
import jax.numpy as jnp
from jax import lax
from jax.experimental import pallas as pl
from jax.experimental.pallas import tpu as pltpu
from jax.sharding import PartitionSpec as P

HEAD = 64
GROUPS = 32
STEPS = 2
LANES = 128
ROW_BLOCK = 64
VMEM_LIMIT = 24 * 2**20

guide_weight = 5.0
norm_eps = 1e-06


VMEM = pl.BlockSpec(memory_space=pltpu.VMEM)
SMEM = pl.BlockSpec(memory_space=pltpu.SMEM)
ANY = pl.BlockSpec(memory_space=pl.ANY)


def near(x):
    return pltpu.with_memory_space_constraint(x, pltpu.VMEM)


def stay(x):
    return pltpu.with_memory_space_constraint(x, pltpu.HBM)


def alpha_bars(t_ref):
    shape = (8, LANES)
    grid = lax.broadcasted_iota(jnp.int32, shape, 0) * LANES + lax.broadcasted_iota(
        jnp.int32, shape, 1
    )
    ramp = grid.astype(jnp.float32) / 999.0
    root = math.sqrt(0.00085) + ramp * (math.sqrt(0.012) - math.sqrt(0.00085))
    logs = jnp.log1p(-root * root)

    def alpha_bar(t):
        picked = jnp.where(grid <= t, logs, 0.0)
        return jnp.exp(jnp.sum(jnp.sum(picked, axis=1, keepdims=True), axis=0, keepdims=True))

    return [alpha_bar(t_ref[k]) for k in range(STEPS + 1)]


def sampler_weights(bars, k):
    keep = jnp.sqrt(bars[k + 1] / bars[k])
    push = jnp.sqrt(1.0 - bars[k + 1]) - keep * jnp.sqrt(1.0 - bars[k])
    return keep, push


def split3(x):
    hi = x.astype(jnp.bfloat16)
    rest = x - hi.astype(jnp.float32)
    mid = rest.astype(jnp.bfloat16)
    low = (rest - mid.astype(jnp.float32)).astype(jnp.bfloat16)
    return [hi.astype(jnp.float32), mid.astype(jnp.float32), low.astype(jnp.float32)]


def stack8(rows):
    pad = jnp.zeros((8 - len(rows),) + rows[0].shape[1:], jnp.float32)
    return jnp.concatenate(list(rows) + [pad], axis=0).astype(jnp.bfloat16)


def norm_factors(state, gain):
    rows, width = state.shape
    per = width // GROUPS
    sums = jnp.sum(state, axis=0, keepdims=True)
    squares = jnp.sum(state * state, axis=0, keepdims=True)
    channel = lax.broadcasted_iota(jnp.int32, (width, LANES), 0)
    first = lax.broadcasted_iota(jnp.int32, (width, LANES), 1) * per
    member = ((channel >= first) & (channel < first + per)).astype(jnp.float32).astype(jnp.bfloat16)
    parts = jnp.dot(
        stack8(split3(sums) + split3(squares)), member, preferred_element_type=jnp.float32
    )
    count = float(rows * per)
    mean = (parts[0:1] + parts[1:2] + parts[2:3]) / count
    square = (parts[3:4] + parts[4:5] + parts[5:6]) / count
    scale = lax.rsqrt(square - mean * mean + norm_eps)
    channel_t = lax.broadcasted_iota(jnp.int32, (LANES, width), 1)
    first_t = lax.broadcasted_iota(jnp.int32, (LANES, width), 0) * per
    member_t = ((channel_t >= first_t) & (channel_t < first_t + per)).astype(jnp.float32)
    lane = lax.broadcasted_iota(jnp.int32, (1, LANES), 1)
    scale = jnp.where(lane < GROUPS, scale, 0.0)
    wide = jnp.dot(
        stack8(split3(mean) + split3(scale)),
        member_t.astype(jnp.bfloat16),
        preferred_element_type=jnp.float32,
    )
    mean_c = wide[0:1] + wide[1:2] + wide[2:3]
    scale_c = wide[3:4] + wide[4:5] + wide[5:6]
    return mean_c, scale_c * gain


def dot_t(a, b):
    return lax.dot_general(a, b, (((1,), (1,)), ((), ())), preferred_element_type=jnp.float32)


def weigh(scores, allowed, values):
    if allowed is not None:
        scores = jnp.where(allowed, scores, -1e30)
    top = jnp.max(scores, axis=-1, keepdims=True)
    weights = jnp.exp(scores - top)
    total = jnp.sum(weights, axis=-1, keepdims=True)
    acc = jnp.dot(weights.astype(jnp.bfloat16), values, preferred_element_type=jnp.float32)
    return top, total, acc


def block_of(index, size):
    if size & (size - 1) == 0:
        return lax.shift_right_logical(index, size.bit_length() - 1)
    return index // size


def attend(q, keys, values, texts, ctx, guides, own_mask):
    rows, width = q.shape
    out = []
    for low in range(0, width, LANES):
        cut = slice(low, min(low + LANES, width))
        wide = cut.stop - cut.start
        heads = wide // HEAD
        qc = q[:, cut]
        lane = lax.broadcasted_iota(jnp.int32, (rows, wide), 1)
        picks = [(lane >= HEAD * h) & (lane < HEAD * (h + 1)) for h in range(heads)]
        stacked = jnp.concatenate([jnp.where(pick, qc, 0.0) for pick in picks], axis=0)
        stacked = stacked.astype(jnp.bfloat16)
        scores = dot_t(stacked, keys[:, cut])
        allowed = None
        if own_mask is not None:
            allowed = jnp.concatenate([own_mask] * heads, axis=0)
        top, total, acc = weigh(scores, allowed, values[:, cut])
        halves = []
        for tk, tv in texts:
            text_scores = dot_t(stacked, tk[:, cut])
            seen = lax.broadcasted_iota(jnp.int32, text_scores.shape, 1) < ctx
            halves.append(weigh(text_scores, seen, tv[:, cut]))
        near = 0.0
        mixed = 0.0
        for (t_top, t_total, t_acc), guide in zip(halves, guides):
            both = jnp.maximum(top, t_top)
            fade = jnp.exp(top - both)
            t_fade = jnp.exp(t_top - both)
            share = guide / (total * fade + t_total * t_fade)
            near = near + fade * share
            mixed = mixed + t_acc * (t_fade * share)
        mixed = mixed + acc * near
        piece = mixed[:rows]
        for h in range(1, heads):
            piece = jnp.where(picks[h], mixed[h * rows : (h + 1) * rows], piece)
        out.append(piece.astype(jnp.bfloat16))
    return out


def prepare_kernel(images, refs):
    keys, values, text_k, text_v, kv_out, txt_out = refs
    c = lax.axis_index("cfg")
    for i in range(images):
        kv_out[0, i] = keys[c * images + i]
        kv_out[1, i] = values[c * images + i]
    ctx, width = text_k.shape[1:]
    pad = jnp.zeros((txt_out.shape[1] - ctx, width), jnp.float32)
    for n, ref in enumerate((text_k, text_v)):
        rows = jnp.concatenate([ref[0].astype(jnp.float32), pad], axis=0)
        txt_out[n] = rows.astype(jnp.bfloat16)


def load_kernel(count, refs):
    sources, targets, sems = refs[:count], refs[count : 2 * count], refs[2 * count]
    copies = [
        pltpu.make_async_copy(src, dst, sems.at[n])
        for n, (src, dst) in enumerate(zip(sources, targets))
    ]
    for copy in copies:
        copy.start()
    for copy in copies:
        copy.wait()


def guidance():
    first = lax.axis_index("cfg") == 0
    return (
        jnp.where(first, guide_weight, 1.0 - guide_weight),
        jnp.where(first, 1.0 - guide_weight, guide_weight),
    )


def is_keeper(images):
    mine = lax.axis_index("batch") // images if images > 1 else lax.axis_index("batch")
    return mine == lax.axis_index("cfg")


def first_kernel(images, patches, ctx, refs):
    (t_ref, wq, wk, wv, wo, gain, bias, txt_a, txt_b, kv_own, lat_here) = refs[:11]
    n = 11
    lats = refs[n : n + images * patches]
    n += images * patches
    kvs = refs[n : n + patches - 1]
    n += patches - 1
    base, send, k_out, v_out, samp = refs[n : n + 5]
    state_s, normed_s, q_s, key_s, val_s, att_s = refs[n + 5 :]
    tok = lat_here.shape[1]
    rows = tok * patches
    bars = alpha_bars(t_ref)
    for k in range(STEPS):
        for n_row, value in enumerate(sampler_weights(bars, k)):
            at = 2 * k + n_row
            samp[at : at + 1, :] = jnp.broadcast_to(value, (1, LANES))
    keep, push = sampler_weights(bars, 0)
    keeper = is_keeper(images)
    guides = guidance()
    texts = ((txt_a.at[0], txt_a.at[1]), (txt_b.at[0], txt_b.at[1]))
    for i in range(images):
        own = lats[i * patches][...]
        if images == 1:
            own = jnp.where(keeper, lat_here[0], own)
        state_s[0:tok, :] = own
        for k in range(1, patches):
            state_s[k * tok : (k + 1) * tok, :] = lats[i * patches + k][...]
        mean, factor = norm_factors(state_s[...], gain[...].reshape(1, -1))
        normed_s[...] = ((state_s[...] - mean) * factor + bias[...].reshape(1, -1)).astype(
            jnp.bfloat16
        )
        normed = normed_s[...]
        q_s[...] = (
            jnp.dot(normed, wq[...], preferred_element_type=jnp.float32)
            .astype(jnp.bfloat16)
            .astype(jnp.float32)
            * HEAD ** (-0.5)
        )
        fresh = jnp.dot(normed, wk[...], preferred_element_type=jnp.float32).astype(jnp.bfloat16)
        key_s[rows : 2 * rows, :] = fresh
        k_out[i] = fresh
        fresh = jnp.dot(normed, wv[...], preferred_element_type=jnp.float32).astype(jnp.bfloat16)
        val_s[rows : 2 * rows, :] = fresh
        v_out[i] = fresh
        key_s[0:tok, :] = kv_own[0, i]
        val_s[0:tok, :] = kv_own[1, i]
        for k in range(1, patches):
            key_s[k * tok : (k + 1) * tok, :] = kvs[k - 1][0, i]
            val_s[k * tok : (k + 1) * tok, :] = kvs[k - 1][1, i]

        def block(start, size):
            row = lax.broadcasted_iota(jnp.int32, (size, 2 * rows), 0) + start
            col = lax.broadcasted_iota(jnp.int32, (size, 2 * rows), 1)
            fresh_col = col >= rows
            same = block_of(row, tok) == block_of(jnp.where(fresh_col, col - rows, col), tok)
            mask = same == fresh_col
            pieces = attend(
                q_s[pl.ds(start, size), :], key_s, val_s, texts, ctx, guides, mask
            )
            for n_piece, piece in enumerate(pieces):
                at = n_piece * LANES
                att_s[pl.ds(start, size), at : at + piece.shape[1]] = piece

        size = min(rows, ROW_BLOCK)
        if rows % size:
            size = tok
        if rows == size:
            block(0, rows)
        else:

            def step(j, carry):
                block(pl.multiple_of(j * size, size), size)
                return carry

            lax.fori_loop(0, rows // size, step, 0)
        part = push * jnp.dot(att_s[...], wo[...], preferred_element_type=jnp.float32)
        send[i] = part.astype(jnp.bfloat16)
        base[i] = (keep + push) * state_s[...] + part


def last_kernel(images, patches, ctx, peers, refs):
    (wq, wk, wv, wo, samp, gain, bias, txt_a, txt_b, base, k_old, v_old) = refs[:12]
    n = 12
    others = refs[n : n + peers]
    n += peers
    base_out, part_out, ring_out, kv_out = refs[n : n + 4]
    state_s, key_s, val_s = refs[n + 4 :]
    rows = state_s.shape[0]
    tok = rows // patches
    keep = samp[2:3, 0:1]
    push = samp[3:4, 0:1]
    guides = guidance()
    texts = ((txt_a.at[0], txt_a.at[1]), (txt_b.at[0], txt_b.at[1]))
    for i in range(images):
        state = base[i]
        for other in others:
            state = state + other[i].astype(jnp.float32)
        state_s[...] = state
        mean, factor = norm_factors(state_s[...], gain[...].reshape(1, -1))
        own = state_s[0:tok, :]
        normed = ((own - mean) * factor + bias[...].reshape(1, -1)).astype(jnp.bfloat16)
        q = (
            jnp.dot(normed, wq[...], preferred_element_type=jnp.float32)
            .astype(jnp.bfloat16)
            .astype(jnp.float32)
            * HEAD ** (-0.5)
        )
        fresh = jnp.dot(normed, wk[...], preferred_element_type=jnp.float32).astype(jnp.bfloat16)
        key_s[0:tok, :] = fresh
        kv_out[0, i] = fresh
        fresh = jnp.dot(normed, wv[...], preferred_element_type=jnp.float32).astype(jnp.bfloat16)
        val_s[0:tok, :] = fresh
        kv_out[1, i] = fresh
        key_s[tok:rows, :] = k_old[i, tok:rows, :]
        val_s[tok:rows, :] = v_old[i, tok:rows, :]
        pieces = attend(q, key_s, val_s, texts, ctx, guides, None)
        att = jnp.concatenate(pieces, axis=1)
        part = push * jnp.dot(att, wo[...], preferred_element_type=jnp.float32)
        part_out[i] = part
        kept = (keep + push) * own + part
        base_out[i] = kept
        ring_out[i] = jnp.where(is_keeper(images), kept, part)


def end_kernel(images, extra, refs):
    base, ring, diag, kv, kv_far = refs[:5]
    others = refs[5 : 5 + 2 * extra]
    latent, keys, values = refs[5 + 2 * extra :]
    keeper = is_keeper(images)
    total = ring[...] + jnp.where(keeper, base[...], diag[...])
    for r in range(extra):
        total = total + jnp.where(keeper, others[2 * r][...], others[2 * r + 1][...])
    latent[0] = total
    c = lax.axis_index("cfg")
    for i in range(images):
        keys[c * images + i] = kv[0, i]
        values[c * images + i] = kv[1, i]
        keys[(1 - c) * images + i] = kv_far[0, i]
        values[(1 - c) * images + i] = kv_far[1, i]


def kernel_call(body, name, args, outs, scratch, scalars=0, far=0, sems=0, final=False):
    def run(*refs):
        body(refs)

    return pl.pallas_call(
        run,
        out_shape=[
            jax.ShapeDtypeStruct(s, d) if final else pltpu.VMEM(s, d) for s, d in outs
        ],
        in_specs=[SMEM] * scalars + [ANY] * far + [VMEM] * (len(args) - scalars - far),
        out_specs=[VMEM] * len(outs),
        scratch_shapes=([pltpu.SemaphoreType.DMA((sems,))] if sems else [])
        + [pltpu.VMEM(s, d) for s, d in scratch],
        compiler_params=pltpu.CompilerParams(vmem_limit_bytes=VMEM_LIMIT),
        name=name,
    )(*args)


class Grid:
    def __init__(self, mesh):
        self.axes = ("patch", "cfg", "batch")
        self.sizes = tuple(mesh.shape[a] for a in self.axes)

    def flat(self, p, c, b):
        return (p * self.sizes[1] + c) * self.sizes[2] + b

    def pull(self, x, source):
        pairs = []
        for p in range(self.sizes[0]):
            for c in range(self.sizes[1]):
                for b in range(self.sizes[2]):
                    src = source(p, c, b)
                    if src is not None and src != (p, c, b):
                        pairs.append((self.flat(*src), self.flat(p, c, b)))
        return lax.ppermute(x, self.axes, pairs)


def pick(stack, index):
    if len(stack) == 1:
        return stack[0]
    return lax.dynamic_index_in_dim(jnp.stack(stack), index, 0, keepdims=False)


def body(
    grid,
    latent,
    stale_keys,
    stale_values,
    text_keys,
    text_values,
    w_query,
    w_key,
    w_value,
    w_out,
    norm_gain,
    norm_bias,
    timesteps,
):
    patches, halves, batch = grid.sizes
    state = latent[0]
    tok, width = state.shape
    images = stale_keys.shape[0]
    mine = images // halves
    local = w_query.shape[1]
    ctx = text_keys.shape[1]
    ctx_pad = -(-ctx // 16) * 16
    rows = tok * patches
    b = lax.axis_index("batch")

    def away(p, s):
        return p ^ s if patches & (patches - 1) == 0 else (p - s) % patches

    def other_core(p, cc, bb):
        return (p, 1 - cc, bb)

    def latent_source(k, s):
        def source(p, cc, bb):
            if mine == 1 and s == 0:
                return (p, 1 - cc, 1 - bb)
            x = cc * mine + (bb + k) % mine
            return (away(p, s), cc if bb // mine == cc else 1 - cc, x)

        return source

    slots = [[grid.pull(state, latent_source(k, s)) for s in range(patches)] for k in range(mine)]
    if mine > 1:
        slots[0][0] = jnp.where(is_keeper(mine), state, slots[0][0])
    lat = [
        pick([slots[k][s] for k in range(mine)], (i - b) % mine)
        for i in range(mine)
        for s in range(patches)
    ]
    kv_own, txt_own = kernel_call(
        functools.partial(prepare_kernel, mine),
        "prepare",
        [stay(x) for x in (stale_keys, stale_values, text_keys, text_values)],
        [((2, mine, tok, local), jnp.bfloat16), ((2, ctx_pad, local), jnp.bfloat16)],
        [],
    )
    kvs = [
        grid.pull(kv_own, lambda p, cc, bb, s=s: (away(p, s), cc, bb)) for s in range(1, patches)
    ]
    txt_far = grid.pull(txt_own, other_core)

    weights = [stay(w) for w in (w_query, w_key, w_value, w_out)]
    weights = kernel_call(
        functools.partial(load_kernel, len(weights)),
        "load",
        weights,
        [(w.shape, w.dtype) for w in weights],
        [],
        far=len(weights),
        sems=len(weights),
    )
    weights = [near(w) for w in weights]
    affine = [stay(norm_gain), stay(norm_bias)]
    texts = [near(txt_own), near(txt_far)]
    base, send, k0, v0, samp = kernel_call(
        functools.partial(first_kernel, mine, patches, ctx),
        "first",
        [stay(timesteps)]
        + weights
        + affine
        + texts
        + [near(kv_own), stay(latent)]
        + [near(x) for x in lat + kvs],
        [
            ((mine, rows, width), jnp.float32),
            ((mine, rows, width), jnp.bfloat16),
            ((mine, rows, local), jnp.bfloat16),
            ((mine, rows, local), jnp.bfloat16),
            ((2 * STEPS, LANES), jnp.float32),
        ],
        [
            ((rows, width), jnp.float32),
            ((rows, width), jnp.bfloat16),
            ((rows, local), jnp.float32),
            ((2 * rows, local), jnp.bfloat16),
            ((2 * rows, local), jnp.bfloat16),
            ((rows, local), jnp.bfloat16),
        ],
        scalars=1,
    )
    others = [
        grid.pull(send, lambda p, cc, bb, r=r: (p, cc, (bb + r) % batch)) for r in range(1, batch)
    ]
    base1, part1, ring1, kv1 = kernel_call(
        functools.partial(last_kernel, mine, patches, ctx, batch - 1),
        "last",
        weights
        + [near(samp)]
        + affine
        + texts
        + [near(x) for x in [base, k0, v0] + others],
        [
            ((mine, tok, width), jnp.float32),
            ((mine, tok, width), jnp.float32),
            ((mine, tok, width), jnp.float32),
            ((2, mine, tok, local), jnp.bfloat16),
        ],
        [
            ((rows, width), jnp.float32),
            ((rows, local), jnp.bfloat16),
            ((rows, local), jnp.bfloat16),
        ],
    )

    kv_far = grid.pull(kv1, other_core)
    own_base = pick([base1[i] for i in range(mine)], b % mine)
    ends = []
    for r in [mine] + [r for r in range(1, batch) if r != mine]:
        part = pick([part1[i] for i in range(mine)], ((b - r) % batch) % mine)

        def to_keeper(p, cc, bb, r=r):
            if bb // mine == cc:
                return (p, cc, (bb + r) % batch)
            return (p, 1 - cc, bb) if r == mine else None

        def to_partner(p, cc, bb, r=r):
            if mine == 1:
                return (p, 1 - cc, 1 - bb)
            return None if bb // mine == cc else (p, 1 - cc, (bb + r) % batch)

        sent = part
        if r == mine:
            sent = ring1[0] if mine == 1 else jnp.where(is_keeper(mine), own_base, part)
        ends.append(grid.pull(sent, to_keeper))
        ends.append(grid.pull(part, to_partner))
    final = kernel_call(
        functools.partial(end_kernel, mine, batch - 2),
        "end",
        [near(x) for x in [own_base, ends[0], ends[1], kv1, kv_far] + ends[2:]],
        [
            ((1, tok, width), jnp.float32),
            ((images, tok, local), jnp.bfloat16),
            ((images, tok, local), jnp.bfloat16),
        ],
        [],
        final=True,
    )
    return tuple(final)


def solution(mesh):
    return jax.shard_map(
        functools.partial(body, Grid(mesh)),
        mesh=mesh,
        in_specs=(
            P(("prompts", "batch"), "patch", None),
            P("prompts", "patch", "batch"),
            P("prompts", "patch", "batch"),
            P(("prompts", "cfg"), None, "batch"),
            P(("prompts", "cfg"), None, "batch"),
            P(None, "batch"),
            P(None, "batch"),
            P(None, "batch"),
            P("batch", None),
            P(),
            P(),
            P("prompts"),
        ),
        out_specs=(
            P(("prompts", "batch"), "patch", None),
            P("prompts", "patch", "batch"),
            P("prompts", "patch", "batch"),
        ),
        check_vma=False,
    )
```

```python
import functools
import math

import jax
import jax.numpy as jnp
from jax import lax
from jax.experimental import pallas as pl
from jax.experimental.pallas import tpu as pltpu
from jax.sharding import PartitionSpec as P

HEAD = 64
GROUPS = 32
STEPS = 2
LANES = 128
ROW_BLOCK = 64
VMEM_LIMIT = 24 * 2**20

guide_weight = 5.0
norm_eps = 1e-06


VMEM = pl.BlockSpec(memory_space=pltpu.VMEM)
SMEM = pl.BlockSpec(memory_space=pltpu.SMEM)
ANY = pl.BlockSpec(memory_space=pl.ANY)


def near(x):
    return pltpu.with_memory_space_constraint(x, pltpu.VMEM)


def stay(x):
    return pltpu.with_memory_space_constraint(x, pltpu.HBM)


def alpha_bars(t_ref):
    shape = (8, LANES)
    grid = lax.broadcasted_iota(jnp.int32, shape, 0) * LANES + lax.broadcasted_iota(
        jnp.int32, shape, 1
    )
    ramp = grid.astype(jnp.float32) / 999.0
    root = math.sqrt(0.00085) + ramp * (math.sqrt(0.012) - math.sqrt(0.00085))
    logs = jnp.log1p(-root * root)

    def alpha_bar(t):
        picked = jnp.where(grid <= t, logs, 0.0)
        return jnp.exp(jnp.sum(jnp.sum(picked, axis=1, keepdims=True), axis=0, keepdims=True))

    return [alpha_bar(t_ref[k]) for k in range(STEPS + 1)]


def sampler_weights(bars, k):
    keep = jnp.sqrt(bars[k + 1] / bars[k])
    push = jnp.sqrt(1.0 - bars[k + 1]) - keep * jnp.sqrt(1.0 - bars[k])
    return keep, push


def split3(x):
    hi = x.astype(jnp.bfloat16)
    rest = x - hi.astype(jnp.float32)
    mid = rest.astype(jnp.bfloat16)
    low = (rest - mid.astype(jnp.float32)).astype(jnp.bfloat16)
    return [hi.astype(jnp.float32), mid.astype(jnp.float32), low.astype(jnp.float32)]


def stack8(rows):
    pad = jnp.zeros((8 - len(rows),) + rows[0].shape[1:], jnp.float32)
    return jnp.concatenate(list(rows) + [pad], axis=0).astype(jnp.bfloat16)


def norm_factors(state, gain):
    rows, width = state.shape
    per = width // GROUPS
    sums = jnp.sum(state, axis=0, keepdims=True)
    squares = jnp.sum(state * state, axis=0, keepdims=True)
    channel = lax.broadcasted_iota(jnp.int32, (width, LANES), 0)
    first = lax.broadcasted_iota(jnp.int32, (width, LANES), 1) * per
    member = ((channel >= first) & (channel < first + per)).astype(jnp.float32).astype(jnp.bfloat16)
    parts = jnp.dot(
        stack8(split3(sums) + split3(squares)), member, preferred_element_type=jnp.float32
    )
    count = float(rows * per)
    mean = (parts[0:1] + parts[1:2] + parts[2:3]) / count
    square = (parts[3:4] + parts[4:5] + parts[5:6]) / count
    scale = lax.rsqrt(square - mean * mean + norm_eps)
    channel_t = lax.broadcasted_iota(jnp.int32, (LANES, width), 1)
    first_t = lax.broadcasted_iota(jnp.int32, (LANES, width), 0) * per
    member_t = ((channel_t >= first_t) & (channel_t < first_t + per)).astype(jnp.float32)
    lane = lax.broadcasted_iota(jnp.int32, (1, LANES), 1)
    scale = jnp.where(lane < GROUPS, scale, 0.0)
    wide = jnp.dot(
        stack8(split3(mean) + split3(scale)),
        member_t.astype(jnp.bfloat16),
        preferred_element_type=jnp.float32,
    )
    mean_c = wide[0:1] + wide[1:2] + wide[2:3]
    scale_c = wide[3:4] + wide[4:5] + wide[5:6]
    return mean_c, scale_c * gain


def dot_t(a, b):
    return lax.dot_general(a, b, (((1,), (1,)), ((), ())), preferred_element_type=jnp.float32)


def weigh(scores, allowed, values):
    if allowed is not None:
        scores = jnp.where(allowed, scores, -1e30)
    top = jnp.max(scores, axis=-1, keepdims=True)
    weights = jnp.exp(scores - top)
    total = jnp.sum(weights, axis=-1, keepdims=True)
    acc = jnp.dot(weights.astype(jnp.bfloat16), values, preferred_element_type=jnp.float32)
    return top, total, acc


def block_of(index, size):
    if size & (size - 1) == 0:
        return lax.shift_right_logical(index, size.bit_length() - 1)
    return index // size


def attend(q, keys, values, texts, ctx, guides, own_mask):
    rows, width = q.shape
    out = []
    for low in range(0, width, LANES):
        cut = slice(low, min(low + LANES, width))
        wide = cut.stop - cut.start
        heads = wide // HEAD
        qc = q[:, cut]
        lane = lax.broadcasted_iota(jnp.int32, (rows, wide), 1)
        picks = [(lane >= HEAD * h) & (lane < HEAD * (h + 1)) for h in range(heads)]
        stacked = jnp.concatenate([jnp.where(pick, qc, 0.0) for pick in picks], axis=0)
        stacked = stacked.astype(jnp.bfloat16)
        scores = dot_t(stacked, keys[:, cut])
        allowed = None
        if own_mask is not None:
            allowed = jnp.concatenate([own_mask] * heads, axis=0)
        top, total, acc = weigh(scores, allowed, values[:, cut])
        halves = []
        for tk, tv in texts:
            text_scores = dot_t(stacked, tk[:, cut])
            seen = lax.broadcasted_iota(jnp.int32, text_scores.shape, 1) < ctx
            halves.append(weigh(text_scores, seen, tv[:, cut]))
        near = 0.0
        mixed = 0.0
        for (t_top, t_total, t_acc), guide in zip(halves, guides):
            both = jnp.maximum(top, t_top)
            fade = jnp.exp(top - both)
            t_fade = jnp.exp(t_top - both)
            share = guide / (total * fade + t_total * t_fade)
            near = near + fade * share
            mixed = mixed + t_acc * (t_fade * share)
        mixed = mixed + acc * near
        piece = mixed[:rows]
        for h in range(1, heads):
            piece = jnp.where(picks[h], mixed[h * rows : (h + 1) * rows], piece)
        out.append(piece.astype(jnp.bfloat16))
    return out


def prepare_kernel(images, refs):
    keys, values, text_k, text_v, kv_out, txt_out = refs
    c = lax.axis_index("cfg")
    for i in range(images):
        kv_out[0, i] = keys[c * images + i]
        kv_out[1, i] = values[c * images + i]
    ctx, width = text_k.shape[1:]
    pad = jnp.zeros((txt_out.shape[1] - ctx, width), jnp.float32)
    for n, ref in enumerate((text_k, text_v)):
        rows = jnp.concatenate([ref[0].astype(jnp.float32), pad], axis=0)
        txt_out[n] = rows.astype(jnp.bfloat16)


def load_kernel(count, refs):
    sources, targets, sems = refs[:count], refs[count : 2 * count], refs[2 * count]
    copies = [
        pltpu.make_async_copy(src, dst, sems.at[n])
        for n, (src, dst) in enumerate(zip(sources, targets))
    ]
    for copy in copies:
        copy.start()
    for copy in copies:
        copy.wait()


def guidance():
    first = lax.axis_index("cfg") == 0
    return (
        jnp.where(first, guide_weight, 1.0 - guide_weight),
        jnp.where(first, 1.0 - guide_weight, guide_weight),
    )


def is_keeper(images):
    mine = lax.axis_index("batch") // images if images > 1 else lax.axis_index("batch")
    return mine == lax.axis_index("cfg")


def first_kernel(images, patches, ctx, refs):
    (t_ref, wq, wk, wv, wo, gain, bias, txt_a, txt_b, kv_own, lat_here) = refs[:11]
    n = 11
    lats = refs[n : n + images * patches]
    n += images * patches
    kvs = refs[n : n + patches - 1]
    n += patches - 1
    base, send, k_out, v_out, samp = refs[n : n + 5]
    state_s, normed_s, q_s, key_s, val_s, att_s = refs[n + 5 :]
    tok = lat_here.shape[1]
    rows = tok * patches
    bars = alpha_bars(t_ref)
    for k in range(STEPS):
        for n_row, value in enumerate(sampler_weights(bars, k)):
            at = 2 * k + n_row
            samp[at : at + 1, :] = jnp.broadcast_to(value, (1, LANES))
    keep, push = sampler_weights(bars, 0)
    keeper = is_keeper(images)
    guides = guidance()
    texts = ((txt_a.at[0], txt_a.at[1]), (txt_b.at[0], txt_b.at[1]))
    for i in range(images):
        own = lats[i * patches][...]
        if images == 1:
            own = jnp.where(keeper, lat_here[0], own)
        state_s[0:tok, :] = own
        for k in range(1, patches):
            state_s[k * tok : (k + 1) * tok, :] = lats[i * patches + k][...]
        mean, factor = norm_factors(state_s[...], gain[...].reshape(1, -1))
        normed_s[...] = ((state_s[...] - mean) * factor + bias[...].reshape(1, -1)).astype(
            jnp.bfloat16
        )
        normed = normed_s[...]
        q_s[...] = (
            jnp.dot(normed, wq[...], preferred_element_type=jnp.float32)
            .astype(jnp.bfloat16)
            .astype(jnp.float32)
            * HEAD ** (-0.5)
        )
        fresh = jnp.dot(normed, wk[...], preferred_element_type=jnp.float32).astype(jnp.bfloat16)
        key_s[rows : 2 * rows, :] = fresh
        k_out[i] = fresh
        fresh = jnp.dot(normed, wv[...], preferred_element_type=jnp.float32).astype(jnp.bfloat16)
        val_s[rows : 2 * rows, :] = fresh
        v_out[i] = fresh
        key_s[0:tok, :] = kv_own[0, i]
        val_s[0:tok, :] = kv_own[1, i]
        for k in range(1, patches):
            key_s[k * tok : (k + 1) * tok, :] = kvs[k - 1][0, i]
            val_s[k * tok : (k + 1) * tok, :] = kvs[k - 1][1, i]

        def block(start, size):
            row = lax.broadcasted_iota(jnp.int32, (size, 2 * rows), 0) + start
            col = lax.broadcasted_iota(jnp.int32, (size, 2 * rows), 1)
            fresh_col = col >= rows
            same = block_of(row, tok) == block_of(jnp.where(fresh_col, col - rows, col), tok)
            mask = same == fresh_col
            pieces = attend(
                q_s[pl.ds(start, size), :], key_s, val_s, texts, ctx, guides, mask
            )
            for n_piece, piece in enumerate(pieces):
                at = n_piece * LANES
                att_s[pl.ds(start, size), at : at + piece.shape[1]] = piece

        size = min(rows, ROW_BLOCK)
        if rows % size:
            size = tok
        if rows == size:
            block(0, rows)
        else:

            def step(j, carry):
                block(pl.multiple_of(j * size, size), size)
                return carry

            lax.fori_loop(0, rows // size, step, 0)
        part = push * jnp.dot(att_s[...], wo[...], preferred_element_type=jnp.float32)
        send[i] = part.astype(jnp.bfloat16)
        base[i] = (keep + push) * state_s[...] + part


def last_kernel(images, patches, ctx, peers, refs):
    (wq, wk, wv, wo, samp, gain, bias, txt_a, txt_b, base, k_old, v_old) = refs[:12]
    n = 12
    others = refs[n : n + peers]
    n += peers
    base_out, part_out, ring_out, kv_out = refs[n : n + 4]
    state_s, key_s, val_s = refs[n + 4 :]
    rows = state_s.shape[0]
    tok = rows // patches
    keep = samp[2:3, 0:1]
    push = samp[3:4, 0:1]
    guides = guidance()
    texts = ((txt_a.at[0], txt_a.at[1]), (txt_b.at[0], txt_b.at[1]))
    for i in range(images):
        state = base[i]
        for other in others:
            state = state + other[i].astype(jnp.float32)
        state_s[...] = state
        mean, factor = norm_factors(state_s[...], gain[...].reshape(1, -1))
        own = state_s[0:tok, :]
        normed = ((own - mean) * factor + bias[...].reshape(1, -1)).astype(jnp.bfloat16)
        q = (
            jnp.dot(normed, wq[...], preferred_element_type=jnp.float32)
            .astype(jnp.bfloat16)
            .astype(jnp.float32)
            * HEAD ** (-0.5)
        )
        fresh = jnp.dot(normed, wk[...], preferred_element_type=jnp.float32).astype(jnp.bfloat16)
        key_s[0:tok, :] = fresh
        kv_out[0, i] = fresh
        fresh = jnp.dot(normed, wv[...], preferred_element_type=jnp.float32).astype(jnp.bfloat16)
        val_s[0:tok, :] = fresh
        kv_out[1, i] = fresh
        key_s[tok:rows, :] = k_old[i, tok:rows, :]
        val_s[tok:rows, :] = v_old[i, tok:rows, :]
        pieces = attend(q, key_s, val_s, texts, ctx, guides, None)
        att = jnp.concatenate(pieces, axis=1)
        part = push * jnp.dot(att, wo[...], preferred_element_type=jnp.float32)
        part_out[i] = part
        kept = (keep + push) * own + part
        base_out[i] = kept
        ring_out[i] = jnp.where(is_keeper(images), kept, part)


def end_kernel(images, extra, refs):
    base, ring, diag, kv, kv_far = refs[:5]
    others = refs[5 : 5 + 2 * extra]
    latent, keys, values = refs[5 + 2 * extra :]
    keeper = is_keeper(images)
    total = ring[...] + jnp.where(keeper, base[...], diag[...])
    for r in range(extra):
        total = total + jnp.where(keeper, others[2 * r][...], others[2 * r + 1][...])
    latent[0] = total
    c = lax.axis_index("cfg")
    for i in range(images):
        keys[c * images + i] = kv[0, i]
        values[c * images + i] = kv[1, i]
        keys[(1 - c) * images + i] = kv_far[0, i]
        values[(1 - c) * images + i] = kv_far[1, i]


def kernel_call(body, name, args, outs, scratch, scalars=0, far=0, sems=0, final=False, cost=None):
    def run(*refs):
        body(refs)

    return pl.pallas_call(
        run,
        out_shape=[
            jax.ShapeDtypeStruct(s, d) if final else pltpu.VMEM(s, d) for s, d in outs
        ],
        in_specs=[SMEM] * scalars + [ANY] * far + [VMEM] * (len(args) - scalars - far),
        out_specs=[VMEM] * len(outs),
        scratch_shapes=([pltpu.SemaphoreType.DMA((sems,))] if sems else [])
        + [pltpu.VMEM(s, d) for s, d in scratch],
        compiler_params=pltpu.CompilerParams(vmem_limit_bytes=VMEM_LIMIT),
        cost_estimate=cost,
        name=name,
    )(*args)


class Grid:
    def __init__(self, mesh):
        self.axes = ("patch", "cfg", "batch")
        self.sizes = tuple(mesh.shape[a] for a in self.axes)

    def flat(self, p, c, b):
        return (p * self.sizes[1] + c) * self.sizes[2] + b

    def pull(self, x, source):
        pairs = []
        for p in range(self.sizes[0]):
            for c in range(self.sizes[1]):
                for b in range(self.sizes[2]):
                    src = source(p, c, b)
                    if src is not None and src != (p, c, b):
                        pairs.append((self.flat(*src), self.flat(p, c, b)))
        return lax.ppermute(x, self.axes, pairs)


def pick(stack, index):
    if len(stack) == 1:
        return stack[0]
    return lax.dynamic_index_in_dim(jnp.stack(stack), index, 0, keepdims=False)


def body(
    grid,
    latent,
    stale_keys,
    stale_values,
    text_keys,
    text_values,
    w_query,
    w_key,
    w_value,
    w_out,
    norm_gain,
    norm_bias,
    timesteps,
):
    patches, halves, batch = grid.sizes
    state = latent[0]
    tok, width = state.shape
    images = stale_keys.shape[0]
    mine = images // halves
    local = w_query.shape[1]
    ctx = text_keys.shape[1]
    ctx_pad = -(-ctx // 16) * 16
    rows = tok * patches
    b = lax.axis_index("batch")

    def away(p, s):
        return p ^ s if patches & (patches - 1) == 0 else (p - s) % patches

    def other_core(p, cc, bb):
        return (p, 1 - cc, bb)

    def latent_source(k, s):
        def source(p, cc, bb):
            if mine == 1 and s == 0:
                return (p, 1 - cc, 1 - bb)
            x = cc * mine + (bb + k) % mine
            return (away(p, s), cc if bb // mine == cc else 1 - cc, x)

        return source

    slots = [[grid.pull(state, latent_source(k, s)) for s in range(patches)] for k in range(mine)]
    if mine > 1:
        slots[0][0] = jnp.where(is_keeper(mine), state, slots[0][0])
    lat = [
        pick([slots[k][s] for k in range(mine)], (i - b) % mine)
        for i in range(mine)
        for s in range(patches)
    ]
    kv_own, txt_own = kernel_call(
        functools.partial(prepare_kernel, mine),
        "prepare",
        [stay(x) for x in (stale_keys, stale_values, text_keys, text_values)],
        [((2, mine, tok, local), jnp.bfloat16), ((2, ctx_pad, local), jnp.bfloat16)],
        [],
        cost=pl.CostEstimate(flops=10**10, bytes_accessed=10**8, transcendentals=0),
    )
    kvs = [
        grid.pull(kv_own, lambda p, cc, bb, s=s: (away(p, s), cc, bb)) for s in range(1, patches)
    ]
    txt_far = grid.pull(txt_own, other_core)

    weights = [w_query, w_key, w_value, w_out]
    weights = [near(w) for w in weights]
    affine = [stay(norm_gain), stay(norm_bias)]
    texts = [near(txt_own), near(txt_far)]
    base, send, k0, v0, samp = kernel_call(
        functools.partial(first_kernel, mine, patches, ctx),
        "first",
        [stay(timesteps)]
        + weights
        + affine
        + texts
        + [near(kv_own), stay(latent)]
        + [near(x) for x in lat + kvs],
        [
            ((mine, rows, width), jnp.float32),
            ((mine, rows, width), jnp.bfloat16),
            ((mine, rows, local), jnp.bfloat16),
            ((mine, rows, local), jnp.bfloat16),
            ((2 * STEPS, LANES), jnp.float32),
        ],
        [
            ((rows, width), jnp.float32),
            ((rows, width), jnp.bfloat16),
            ((rows, local), jnp.float32),
            ((2 * rows, local), jnp.bfloat16),
            ((2 * rows, local), jnp.bfloat16),
            ((rows, local), jnp.bfloat16),
        ],
        scalars=1,
    )
    others = [
        grid.pull(send, lambda p, cc, bb, r=r: (p, cc, (bb + r) % batch)) for r in range(1, batch)
    ]
    base1, part1, ring1, kv1 = kernel_call(
        functools.partial(last_kernel, mine, patches, ctx, batch - 1),
        "last",
        weights
        + [near(samp)]
        + affine
        + texts
        + [near(x) for x in [base, k0, v0] + others],
        [
            ((mine, tok, width), jnp.float32),
            ((mine, tok, width), jnp.float32),
            ((mine, tok, width), jnp.float32),
            ((2, mine, tok, local), jnp.bfloat16),
        ],
        [
            ((rows, width), jnp.float32),
            ((rows, local), jnp.bfloat16),
            ((rows, local), jnp.bfloat16),
        ],
    )

    kv_far = grid.pull(kv1, other_core)
    own_base = pick([base1[i] for i in range(mine)], b % mine)
    ends = []
    for r in [mine] + [r for r in range(1, batch) if r != mine]:
        part = pick([part1[i] for i in range(mine)], ((b - r) % batch) % mine)

        def to_keeper(p, cc, bb, r=r):
            if bb // mine == cc:
                return (p, cc, (bb + r) % batch)
            return (p, 1 - cc, bb) if r == mine else None

        def to_partner(p, cc, bb, r=r):
            if mine == 1:
                return (p, 1 - cc, 1 - bb)
            return None if bb // mine == cc else (p, 1 - cc, (bb + r) % batch)

        sent = part
        if r == mine:
            sent = ring1[0] if mine == 1 else jnp.where(is_keeper(mine), own_base, part)
        ends.append(grid.pull(sent, to_keeper))
        ends.append(grid.pull(part, to_partner))
    final = kernel_call(
        functools.partial(end_kernel, mine, batch - 2),
        "end",
        [near(x) for x in [own_base, ends[0], ends[1], kv1, kv_far] + ends[2:]],
        [
            ((1, tok, width), jnp.float32),
            ((images, tok, local), jnp.bfloat16),
            ((images, tok, local), jnp.bfloat16),
        ],
        [],
        final=True,
    )
    return tuple(final)


def solution(mesh):
    return jax.shard_map(
        functools.partial(body, Grid(mesh)),
        mesh=mesh,
        in_specs=(
            P(("prompts", "batch"), "patch", None),
            P("prompts", "patch", "batch"),
            P("prompts", "patch", "batch"),
            P(("prompts", "cfg"), None, "batch"),
            P(("prompts", "cfg"), None, "batch"),
            P(None, "batch"),
            P(None, "batch"),
            P(None, "batch"),
            P("batch", None),
            P(),
            P(),
            P("prompts"),
        ),
        out_specs=(
            P(("prompts", "batch"), "patch", None),
            P("prompts", "patch", "batch"),
            P("prompts", "patch", "batch"),
        ),
        check_vma=False,
    )
```

```python
import functools
import math

import jax
import jax.numpy as jnp
from jax import lax
from jax.experimental import pallas as pl
from jax.experimental.pallas import tpu as pltpu
from jax.sharding import PartitionSpec as P

HEAD = 64
GROUPS = 32
STEPS = 2
LANES = 128
ROW_BLOCK = 64
VMEM_LIMIT = 24 * 2**20
LONG = pl.CostEstimate(flops=10**10, bytes_accessed=10**8, transcendentals=0)

guide_weight = 5.0
norm_eps = 1e-06


VMEM = pl.BlockSpec(memory_space=pltpu.VMEM)
SMEM = pl.BlockSpec(memory_space=pltpu.SMEM)


def near(x):
    return pltpu.with_memory_space_constraint(x, pltpu.VMEM)


def stay(x):
    return pltpu.with_memory_space_constraint(x, pltpu.HBM)


def alpha_bars(t_ref):
    shape = (8, LANES)
    grid = lax.broadcasted_iota(jnp.int32, shape, 0) * LANES + lax.broadcasted_iota(
        jnp.int32, shape, 1
    )
    ramp = grid.astype(jnp.float32) / 999.0
    root = math.sqrt(0.00085) + ramp * (math.sqrt(0.012) - math.sqrt(0.00085))
    logs = jnp.log1p(-root * root)

    def alpha_bar(t):
        picked = jnp.where(grid <= t, logs, 0.0)
        return jnp.exp(jnp.sum(jnp.sum(picked, axis=1, keepdims=True), axis=0, keepdims=True))

    return [alpha_bar(t_ref[k]) for k in range(STEPS + 1)]


def sampler_weights(bars, k):
    keep = jnp.sqrt(bars[k + 1] / bars[k])
    push = jnp.sqrt(1.0 - bars[k + 1]) - keep * jnp.sqrt(1.0 - bars[k])
    return keep, push


def split3(x):
    hi = x.astype(jnp.bfloat16)
    rest = x - hi.astype(jnp.float32)
    mid = rest.astype(jnp.bfloat16)
    low = (rest - mid.astype(jnp.float32)).astype(jnp.bfloat16)
    return [hi.astype(jnp.float32), mid.astype(jnp.float32), low.astype(jnp.float32)]


def stack8(rows):
    pad = jnp.zeros((8 - len(rows),) + rows[0].shape[1:], jnp.float32)
    return jnp.concatenate(list(rows) + [pad], axis=0).astype(jnp.bfloat16)


def norm_factors(state, gain):
    rows, width = state.shape
    per = width // GROUPS
    sums = jnp.sum(state, axis=0, keepdims=True)
    squares = jnp.sum(state * state, axis=0, keepdims=True)
    channel = lax.broadcasted_iota(jnp.int32, (width, LANES), 0)
    first = lax.broadcasted_iota(jnp.int32, (width, LANES), 1) * per
    member = ((channel >= first) & (channel < first + per)).astype(jnp.float32).astype(jnp.bfloat16)
    parts = jnp.dot(
        stack8(split3(sums) + split3(squares)), member, preferred_element_type=jnp.float32
    )
    count = float(rows * per)
    mean = (parts[0:1] + parts[1:2] + parts[2:3]) / count
    square = (parts[3:4] + parts[4:5] + parts[5:6]) / count
    scale = lax.rsqrt(square - mean * mean + norm_eps)
    channel_t = lax.broadcasted_iota(jnp.int32, (LANES, width), 1)
    first_t = lax.broadcasted_iota(jnp.int32, (LANES, width), 0) * per
    member_t = ((channel_t >= first_t) & (channel_t < first_t + per)).astype(jnp.float32)
    lane = lax.broadcasted_iota(jnp.int32, (1, LANES), 1)
    scale = jnp.where(lane < GROUPS, scale, 0.0)
    wide = jnp.dot(
        stack8(split3(mean) + split3(scale)),
        member_t.astype(jnp.bfloat16),
        preferred_element_type=jnp.float32,
    )
    mean_c = wide[0:1] + wide[1:2] + wide[2:3]
    scale_c = wide[3:4] + wide[4:5] + wide[5:6]
    return mean_c, scale_c * gain


def dot_t(a, b):
    return lax.dot_general(a, b, (((1,), (1,)), ((), ())), preferred_element_type=jnp.float32)


def weigh(scores, allowed, values):
    if allowed is not None:
        scores = jnp.where(allowed, scores, -1e30)
    top = jnp.max(scores, axis=-1, keepdims=True)
    weights = jnp.exp(scores - top)
    total = jnp.sum(weights, axis=-1, keepdims=True)
    acc = jnp.dot(weights.astype(jnp.bfloat16), values, preferred_element_type=jnp.float32)
    return top, total, acc


def block_of(index, size):
    if size & (size - 1) == 0:
        return lax.shift_right_logical(index, size.bit_length() - 1)
    return index // size


def attend(q, keys, values, texts, ctx, guides, own_mask):
    rows, width = q.shape
    out = []
    for low in range(0, width, LANES):
        cut = slice(low, min(low + LANES, width))
        wide = cut.stop - cut.start
        heads = wide // HEAD
        qc = q[:, cut].astype(jnp.float32) * HEAD ** (-0.5)
        lane = lax.broadcasted_iota(jnp.int32, (rows, wide), 1)
        picks = [(lane >= HEAD * h) & (lane < HEAD * (h + 1)) for h in range(heads)]
        stacked = jnp.concatenate([jnp.where(pick, qc, 0.0) for pick in picks], axis=0)
        stacked = stacked.astype(jnp.bfloat16)
        scores = dot_t(stacked, keys[:, cut])
        allowed = None
        if own_mask is not None:
            allowed = jnp.concatenate([own_mask] * heads, axis=0)
        top, total, acc = weigh(scores, allowed, values[:, cut])
        halves = []
        for tk, tv in texts:
            text_scores = dot_t(stacked, tk[:, cut])
            seen = lax.broadcasted_iota(jnp.int32, text_scores.shape, 1) < ctx
            halves.append(weigh(text_scores, seen, tv[:, cut]))
        near = 0.0
        mixed = 0.0
        for (t_top, t_total, t_acc), guide in zip(halves, guides):
            both = jnp.maximum(top, t_top)
            fade = jnp.exp(top - both)
            t_fade = jnp.exp(t_top - both)
            share = guide / (total * fade + t_total * t_fade)
            near = near + fade * share
            mixed = mixed + t_acc * (t_fade * share)
        mixed = mixed + acc * near
        piece = mixed[:rows]
        for h in range(1, heads):
            piece = jnp.where(picks[h], mixed[h * rows : (h + 1) * rows], piece)
        out.append(piece.astype(jnp.bfloat16))
    return out


def packed_rows(tok, width):
    chunks = width // LANES
    return chunks * tok, -(-2 * chunks // 8) * 8


def pack_latent(lat, out):
    tok, width = lat.shape
    body_rows, mean_rows = packed_rows(tok, width)
    mean = jnp.sum(lat, axis=0, keepdims=True) / float(tok)
    hi = mean.astype(jnp.bfloat16).astype(jnp.float32)
    lo = (mean - hi).astype(jnp.bfloat16).astype(jnp.float32)
    diff = lat - (hi + lo)
    cuts = [slice(at, at + LANES) for at in range(0, width, LANES)]
    for n, cut in enumerate(cuts):
        out[n * tok : (n + 1) * tok, :] = diff[:, cut].astype(jnp.bfloat16)
    rows = [hi[:, cut] for cut in cuts] + [lo[:, cut] for cut in cuts]
    if len(rows) < mean_rows:
        rows.append(jnp.zeros((mean_rows - len(rows), LANES), jnp.float32))
    out[body_rows:, :] = jnp.concatenate(rows, axis=0).astype(jnp.bfloat16)


def unpack_latent(packed, target, start, tok):
    width = target.shape[1]
    body_rows, _ = packed_rows(tok, width)
    chunks = width // LANES
    means = packed[body_rows:, :].astype(jnp.float32)
    for n in range(chunks):
        mean = means[n : n + 1] + means[chunks + n : chunks + n + 1]
        diff = packed[n * tok : (n + 1) * tok, :].astype(jnp.float32)
        target[start : start + tok, n * LANES : (n + 1) * LANES] = diff + mean


def prepare_kernel(images, refs):
    keys, values, text_k, text_v, lat, kv_out, txt_out, lat_out = refs
    c = lax.axis_index("cfg")
    pack_latent(lat[0], lat_out)
    for i in range(images):
        kv_out[0, i] = keys[c * images + i]
        kv_out[1, i] = values[c * images + i]
    ctx, width = text_k.shape[1:]
    pad = jnp.zeros((txt_out.shape[1] - ctx, width), jnp.float32)
    for n, ref in enumerate((text_k, text_v)):
        rows = jnp.concatenate([ref[0].astype(jnp.float32), pad], axis=0)
        txt_out[n] = rows.astype(jnp.bfloat16)


def guidance():
    first = lax.axis_index("cfg") == 0
    return (
        jnp.where(first, guide_weight, 1.0 - guide_weight),
        jnp.where(first, 1.0 - guide_weight, guide_weight),
    )


def is_keeper(images):
    mine = lax.axis_index("batch") // images if images > 1 else lax.axis_index("batch")
    return mine == lax.axis_index("cfg")


def project(normed, weight):
    return jnp.dot(normed, weight[...], preferred_element_type=jnp.float32).astype(jnp.bfloat16)


def first_project(images, patches, refs):
    (t_ref, wq, wk, wv, gain, bias, lat_here) = refs[:7]
    n = 7
    lats = refs[n : n + images * patches]
    state_s, q_out, k_out, v_out, samp = refs[n + images * patches :]
    tok = lat_here.shape[1]
    bars = alpha_bars(t_ref)
    for k in range(STEPS):
        for n_row, value in enumerate(sampler_weights(bars, k)):
            at = 2 * k + n_row
            samp[at : at + 1, :] = jnp.broadcast_to(value, (1, LANES))
    keeper = is_keeper(images)
    for i in range(images):
        own = lats[i * patches][...]
        if images == 1:
            own = jnp.where(keeper, lat_here[0], own)
        state_s[i, 0:tok, :] = own
        for k in range(1, patches):
            unpack_latent(lats[i * patches + k], state_s.at[i], k * tok, tok)
        state = state_s[i]
        mean, factor = norm_factors(state, gain[...].reshape(1, -1))
        normed = ((state - mean) * factor + bias[...].reshape(1, -1)).astype(jnp.bfloat16)
        q_out[i] = project(normed, wq)
        k_out[i] = project(normed, wk)
        v_out[i] = project(normed, wv)


def first_attend(images, patches, ctx, refs):
    (samp, wo, txt_a, txt_b, kv_own, state, q, k_new, v_new) = refs[:9]
    n = 9
    kvs = refs[n : n + patches - 1]
    base, send, key_s, val_s, att_s = refs[n + patches - 1 :]
    rows = state.shape[1]
    tok = rows // patches
    keep = samp[0:1, 0:1]
    push = samp[1:2, 0:1]
    guides = guidance()
    texts = ((txt_a.at[0], txt_a.at[1]), (txt_b.at[0], txt_b.at[1]))
    for i in range(images):
        key_s[rows : 2 * rows, :] = k_new[i]
        val_s[rows : 2 * rows, :] = v_new[i]
        key_s[0:tok, :] = kv_own[0, i]
        val_s[0:tok, :] = kv_own[1, i]
        for k in range(1, patches):
            key_s[k * tok : (k + 1) * tok, :] = kvs[k - 1][0, i]
            val_s[k * tok : (k + 1) * tok, :] = kvs[k - 1][1, i]

        def block(start, size):
            row = lax.broadcasted_iota(jnp.int32, (size, 2 * rows), 0) + start
            col = lax.broadcasted_iota(jnp.int32, (size, 2 * rows), 1)
            fresh_col = col >= rows
            same = block_of(row, tok) == block_of(jnp.where(fresh_col, col - rows, col), tok)
            mask = same == fresh_col
            pieces = attend(
                q[i, pl.ds(start, size), :], key_s, val_s, texts, ctx, guides, mask
            )
            for n_piece, piece in enumerate(pieces):
                at = n_piece * LANES
                att_s[pl.ds(start, size), at : at + piece.shape[1]] = piece

        size = min(rows, ROW_BLOCK)
        if rows % size:
            size = tok
        if rows == size:
            block(0, rows)
        else:

            def step(j, carry):
                block(pl.multiple_of(j * size, size), size)
                return carry

            lax.fori_loop(0, rows // size, step, 0)
        part = push * jnp.dot(att_s[...], wo[...], preferred_element_type=jnp.float32)
        send[i] = part.astype(jnp.bfloat16)
        base[i] = (keep + push) * state[i] + part


def last_project(images, patches, peers, refs):
    (wq, wk, wv, gain, bias, base) = refs[:6]
    others = refs[6 : 6 + peers]
    own_out, q_out, kv_out, state_s = refs[6 + peers :]
    rows = state_s.shape[0]
    tok = rows // patches
    for i in range(images):
        state = base[i]
        for other in others:
            state = state + other[i].astype(jnp.float32)
        state_s[...] = state
        mean, factor = norm_factors(state_s[...], gain[...].reshape(1, -1))
        own = state_s[0:tok, :]
        own_out[i] = own
        normed = ((own - mean) * factor + bias[...].reshape(1, -1)).astype(jnp.bfloat16)
        q_out[i] = project(normed, wq)
        kv_out[0, i] = project(normed, wk)
        kv_out[1, i] = project(normed, wv)


def last_attend(images, ctx, refs):
    (samp, wo, txt_a, txt_b, own, q, kv_new, k_old, v_old) = refs[:9]
    base_out, part_out, ring_out, key_s, val_s = refs[9:]
    rows = key_s.shape[0]
    tok = own.shape[1]
    keep = samp[2:3, 0:1]
    push = samp[3:4, 0:1]
    guides = guidance()
    texts = ((txt_a.at[0], txt_a.at[1]), (txt_b.at[0], txt_b.at[1]))
    for i in range(images):
        key_s[0:tok, :] = kv_new[0, i]
        val_s[0:tok, :] = kv_new[1, i]
        key_s[tok:rows, :] = k_old[i, tok:rows, :]
        val_s[tok:rows, :] = v_old[i, tok:rows, :]
        pieces = attend(q[i], key_s, val_s, texts, ctx, guides, None)
        att = jnp.concatenate(pieces, axis=1)
        part = push * jnp.dot(att, wo[...], preferred_element_type=jnp.float32)
        part_out[i] = part
        kept = (keep + push) * own[i] + part
        base_out[i] = kept
        ring_out[i] = jnp.where(is_keeper(images), kept, part)


def end_kernel(images, extra, refs):
    base, ring, diag, kv, kv_far = refs[:5]
    others = refs[5 : 5 + 2 * extra]
    latent, keys, values = refs[5 + 2 * extra :]
    keeper = is_keeper(images)
    total = ring[...] + jnp.where(keeper, base[...], diag[...])
    for r in range(extra):
        total = total + jnp.where(keeper, others[2 * r][...], others[2 * r + 1][...])
    latent[0] = total
    c = lax.axis_index("cfg")
    for i in range(images):
        keys[c * images + i] = kv[0, i]
        values[c * images + i] = kv[1, i]
        keys[(1 - c) * images + i] = kv_far[0, i]
        values[(1 - c) * images + i] = kv_far[1, i]


def kernel_call(body, name, args, outs, scratch, scalars=0, final=False, cost=None):
    def run(*refs):
        body(refs)

    return pl.pallas_call(
        run,
        out_shape=[
            jax.ShapeDtypeStruct(s, d) if final else pltpu.VMEM(s, d) for s, d in outs
        ],
        in_specs=[SMEM] * scalars + [VMEM] * (len(args) - scalars),
        out_specs=[VMEM] * len(outs),
        scratch_shapes=[pltpu.VMEM(s, d) for s, d in scratch],
        compiler_params=pltpu.CompilerParams(vmem_limit_bytes=VMEM_LIMIT),
        cost_estimate=cost,
        name=name,
    )(*args)


class Grid:
    def __init__(self, mesh):
        self.axes = ("patch", "cfg", "batch")
        self.sizes = tuple(mesh.shape[a] for a in self.axes)

    def flat(self, p, c, b):
        return (p * self.sizes[1] + c) * self.sizes[2] + b

    def pull(self, x, source):
        pairs = []
        for p in range(self.sizes[0]):
            for c in range(self.sizes[1]):
                for b in range(self.sizes[2]):
                    src = source(p, c, b)
                    if src is not None and src != (p, c, b):
                        pairs.append((self.flat(*src), self.flat(p, c, b)))
        return lax.ppermute(x, self.axes, pairs)


def pick(stack, index):
    if len(stack) == 1:
        return stack[0]
    return lax.dynamic_index_in_dim(jnp.stack(stack), index, 0, keepdims=False)


def body(
    grid,
    latent,
    stale_keys,
    stale_values,
    text_keys,
    text_values,
    w_query,
    w_key,
    w_value,
    w_out,
    norm_gain,
    norm_bias,
    timesteps,
):
    patches, halves, batch = grid.sizes
    state = latent[0]
    tok, width = state.shape
    images = stale_keys.shape[0]
    mine = images // halves
    local = w_query.shape[1]
    ctx = text_keys.shape[1]
    ctx_pad = -(-ctx // 16) * 16
    rows = tok * patches
    b = lax.axis_index("batch")

    def away(p, s):
        return p ^ s if patches & (patches - 1) == 0 else (p - s) % patches

    def other_core(p, cc, bb):
        return (p, 1 - cc, bb)

    def latent_source(k, s):
        def source(p, cc, bb):
            if mine == 1 and s == 0:
                return (p, 1 - cc, 1 - bb)
            x = cc * mine + (bb + k) % mine
            return (away(p, s), cc if bb // mine == cc else 1 - cc, x)

        return source

    kv_own, txt_own, lat_own = kernel_call(
        functools.partial(prepare_kernel, mine),
        "prepare",
        [stay(x) for x in (stale_keys, stale_values, text_keys, text_values, latent)],
        [
            ((2, mine, tok, local), jnp.bfloat16),
            ((2, ctx_pad, local), jnp.bfloat16),
            ((sum(packed_rows(tok, width)), LANES), jnp.bfloat16),
        ],
        [],
        cost=LONG,
    )
    slots = [
        [grid.pull(lat_own if s else state, latent_source(k, s)) for s in range(patches)]
        for k in range(mine)
    ]
    if mine > 1:
        slots[0][0] = jnp.where(is_keeper(mine), state, slots[0][0])
    lat = [
        pick([slots[k][s] for k in range(mine)], (i - b) % mine)
        for i in range(mine)
        for s in range(patches)
    ]
    kvs = [
        grid.pull(kv_own, lambda p, cc, bb, s=s: (away(p, s), cc, bb)) for s in range(1, patches)
    ]
    txt_far = grid.pull(txt_own, other_core)

    qkv = [near(w) for w in (w_query, w_key, w_value)]
    out_weight = near(w_out)
    affine = [stay(norm_gain), stay(norm_bias)]
    texts = [near(txt_own), near(txt_far)]
    full = ((mine, rows, local), jnp.bfloat16)
    state0, q0, k0, v0, samp = kernel_call(
        functools.partial(first_project, mine, patches),
        "first_project",
        [stay(timesteps)] + qkv + affine + [stay(latent)] + [near(x) for x in lat],
        [((mine, rows, width), jnp.float32), full, full, full, ((2 * STEPS, LANES), jnp.float32)],
        [],
        scalars=1,
    )
    base, send = kernel_call(
        functools.partial(first_attend, mine, patches, ctx),
        "first_attend",
        [near(samp), out_weight]
        + texts
        + [near(x) for x in [kv_own, state0, q0, k0, v0] + kvs],
        [((mine, rows, width), jnp.float32), ((mine, rows, width), jnp.bfloat16)],
        [
            ((2 * rows, local), jnp.bfloat16),
            ((2 * rows, local), jnp.bfloat16),
            ((rows, local), jnp.bfloat16),
        ],
    )
    others = [
        grid.pull(send, lambda p, cc, bb, r=r: (p, cc, (bb + r) % batch)) for r in range(1, batch)
    ]
    own1, q1, kv1 = kernel_call(
        functools.partial(last_project, mine, patches, batch - 1),
        "last_project",
        qkv + affine + [near(x) for x in [base] + others],
        [
            ((mine, tok, width), jnp.float32),
            ((mine, tok, local), jnp.bfloat16),
            ((2, mine, tok, local), jnp.bfloat16),
        ],
        [((rows, width), jnp.float32)],
    )
    kv_far = grid.pull(kv1, other_core)
    base1, part1, ring1 = kernel_call(
        functools.partial(last_attend, mine, ctx),
        "last_attend",
        [near(samp), out_weight] + texts + [near(x) for x in [own1, q1, kv1, k0, v0]],
        [((mine, tok, width), jnp.float32)] * 3,
        [((rows, local), jnp.bfloat16), ((rows, local), jnp.bfloat16)],
        cost=LONG,
    )

    own_base = pick([base1[i] for i in range(mine)], b % mine)
    ends = []
    for r in [mine] + [r for r in range(1, batch) if r != mine]:
        part = pick([part1[i] for i in range(mine)], ((b - r) % batch) % mine)

        def to_keeper(p, cc, bb, r=r):
            if bb // mine == cc:
                return (p, cc, (bb + r) % batch)
            return (p, 1 - cc, bb) if r == mine else None

        def to_partner(p, cc, bb, r=r):
            if mine == 1:
                return (p, 1 - cc, 1 - bb)
            return None if bb // mine == cc else (p, 1 - cc, (bb + r) % batch)

        sent = part
        if r == mine:
            sent = ring1[0] if mine == 1 else jnp.where(is_keeper(mine), own_base, part)
        ends.append(grid.pull(sent, to_keeper))
        ends.append(grid.pull(part, to_partner))
    final = kernel_call(
        functools.partial(end_kernel, mine, batch - 2),
        "end",
        [near(x) for x in [own_base, ends[0], ends[1], kv1, kv_far] + ends[2:]],
        [
            ((1, tok, width), jnp.float32),
            ((images, tok, local), jnp.bfloat16),
            ((images, tok, local), jnp.bfloat16),
        ],
        [],
        final=True,
    )
    return tuple(final)


def solution(mesh):
    return jax.shard_map(
        functools.partial(body, Grid(mesh)),
        mesh=mesh,
        in_specs=(
            P(("prompts", "batch"), "patch", None),
            P("prompts", "patch", "batch"),
            P("prompts", "patch", "batch"),
            P(("prompts", "cfg"), None, "batch"),
            P(("prompts", "cfg"), None, "batch"),
            P(None, "batch"),
            P(None, "batch"),
            P(None, "batch"),
            P("batch", None),
            P(),
            P(),
            P("prompts"),
        ),
        out_specs=(
            P(("prompts", "batch"), "patch", None),
            P("prompts", "patch", "batch"),
            P("prompts", "patch", "batch"),
        ),
        check_vma=False,
    )
```

```python
import functools
import math

import jax
import jax.numpy as jnp
from jax import lax
from jax.experimental import pallas as pl
from jax.experimental.pallas import tpu as pltpu
from jax.sharding import PartitionSpec as P


HEAD = 64
GROUPS = 32
STEPS = 2
LANES = 128
ROW_BLOCK = 64
VMEM_LIMIT = 24 * 2**20
LONG = pl.CostEstimate(flops=10**10, bytes_accessed=10**8, transcendentals=0)

guide_weight = 5.0
norm_eps = 1e-06


VMEM = pl.BlockSpec(memory_space=pltpu.VMEM)
SMEM = pl.BlockSpec(memory_space=pltpu.SMEM)


def near(x):
    return pltpu.with_memory_space_constraint(x, pltpu.VMEM)


def stay(x):
    return pltpu.with_memory_space_constraint(x, pltpu.HBM)


def alpha_bars(t_ref):
    shape = (8, LANES)
    grid = lax.broadcasted_iota(jnp.int32, shape, 0) * LANES + lax.broadcasted_iota(
        jnp.int32, shape, 1
    )
    ramp = grid.astype(jnp.float32) / 999.0
    root = math.sqrt(0.00085) + ramp * (math.sqrt(0.012) - math.sqrt(0.00085))
    logs = jnp.log1p(-root * root)

    def alpha_bar(t):
        picked = jnp.where(grid <= t, logs, 0.0)
        return jnp.exp(jnp.sum(jnp.sum(picked, axis=1, keepdims=True), axis=0, keepdims=True))

    return [alpha_bar(t_ref[k]) for k in range(STEPS + 1)]


def sampler_weights(bars, k):
    keep = jnp.sqrt(bars[k + 1] / bars[k])
    push = jnp.sqrt(1.0 - bars[k + 1]) - keep * jnp.sqrt(1.0 - bars[k])
    return keep, push


def split3(x):
    hi = x.astype(jnp.bfloat16)
    rest = x - hi.astype(jnp.float32)
    mid = rest.astype(jnp.bfloat16)
    low = (rest - mid.astype(jnp.float32)).astype(jnp.bfloat16)
    return [hi.astype(jnp.float32), mid.astype(jnp.float32), low.astype(jnp.float32)]


def stack8(rows):
    pad = jnp.zeros((8 - len(rows),) + rows[0].shape[1:], jnp.float32)
    return jnp.concatenate(list(rows) + [pad], axis=0).astype(jnp.bfloat16)


def group_matrices(width):
    per = width // GROUPS
    out = []
    for shape, axis in (((width, LANES), 0), ((LANES, width), 1)):
        channel = lax.broadcasted_iota(jnp.int32, shape, axis)
        first = lax.broadcasted_iota(jnp.int32, shape, 1 - axis) * per
        member = (channel >= first) & (channel < first + per)
        out.append(member.astype(jnp.float32).astype(jnp.bfloat16))
    return out


def norm_factors(state, gain, member, member_t):
    rows, width = state.shape
    sums = jnp.sum(state, axis=0, keepdims=True)
    squares = jnp.sum(state * state, axis=0, keepdims=True)
    parts = jnp.dot(
        stack8(split3(sums) + split3(squares)), member, preferred_element_type=jnp.float32
    )
    count = float(rows * (width // GROUPS))
    mean = (parts[0:1] + parts[1:2] + parts[2:3]) / count
    square = (parts[3:4] + parts[4:5] + parts[5:6]) / count
    scale = lax.rsqrt(square - mean * mean + norm_eps)
    lane = lax.broadcasted_iota(jnp.int32, (1, LANES), 1)
    scale = jnp.where(lane < GROUPS, scale, 0.0)
    wide = jnp.dot(
        stack8(split3(mean) + split3(scale)), member_t, preferred_element_type=jnp.float32
    )
    mean_c = wide[0:1] + wide[1:2] + wide[2:3]
    scale_c = wide[3:4] + wide[4:5] + wide[5:6]
    return mean_c, scale_c * gain


def dot_t(a, b):
    return lax.dot_general(a, b, (((1,), (1,)), ((), ())), preferred_element_type=jnp.float32)


def soften(scores, allowed):
    if allowed is not None:
        scores = jnp.where(allowed, scores, -1e30)
    top = jnp.max(scores, axis=-1, keepdims=True)
    weights = jnp.exp(scores - top)
    return top, jnp.sum(weights, axis=-1, keepdims=True), weights


def block_of(index, size):
    if size & (size - 1) == 0:
        return lax.shift_right_logical(index, size.bit_length() - 1)
    return index // size


def attend(q, keys, values, texts, ctx, guides, own_mask):
    rows, width = q.shape
    cuts = [slice(low, min(low + LANES, width)) for low in range(0, width, LANES)]
    stacks = []
    for cut in cuts:
        qc = q[:, cut].astype(jnp.float32) * HEAD ** (-0.5)
        lane = lax.broadcasted_iota(jnp.int32, qc.shape, 1)
        heads = qc.shape[1] // HEAD
        picks = [(lane >= HEAD * h) & (lane < HEAD * (h + 1)) for h in range(heads)]
        stacks.append(
            jnp.concatenate([jnp.where(p, qc, 0.0) for p in picks], axis=0).astype(jnp.bfloat16)
        )

    def score(ref):
        return jnp.concatenate([dot_t(st, ref[:, cut]) for st, cut in zip(stacks, cuts)], axis=0)

    allowed = None
    if own_mask is not None:
        allowed = jnp.concatenate([own_mask] * (width // HEAD), axis=0)
    top, total, weights = soften(score(keys), allowed)
    halves = []
    for tk, _ in texts:
        text_scores = score(tk)
        seen = lax.broadcasted_iota(jnp.int32, text_scores.shape, 1) < ctx
        halves.append(soften(text_scores, seen))
    near_share = 0.0
    parts = []
    for (t_top, t_total, t_weights), guide in zip(halves, guides):
        both = jnp.maximum(top, t_top)
        fade = jnp.exp(top - both)
        t_fade = jnp.exp(t_top - both)
        share = guide / (total * fade + t_total * t_fade)
        near_share = near_share + fade * share
        parts.append((t_weights * (t_fade * share)).astype(jnp.bfloat16))
    parts = [(weights * near_share).astype(jnp.bfloat16)] + parts
    sources = [values] + [tv for _, tv in texts]
    out = []
    start = 0
    for cut in cuts:
        heads = (cut.stop - cut.start) // HEAD
        stop = start + heads * rows
        mixed = 0.0
        for part, ref in zip(parts, sources):
            mixed = mixed + jnp.dot(
                part[start:stop], ref[:, cut], preferred_element_type=jnp.float32
            )
        piece = mixed[:rows]
        lane = lax.broadcasted_iota(jnp.int32, piece.shape, 1)
        for h in range(1, heads):
            piece = jnp.where(lane >= HEAD * h, mixed[h * rows : (h + 1) * rows], piece)
        out.append(piece.astype(jnp.bfloat16))
        start = stop
    return out


def packed_rows(tok, width):
    chunks = width // LANES
    return chunks * tok, -(-2 * chunks // 8) * 8


def pack_latent(lat, out):
    tok, width = lat.shape
    body_rows, mean_rows = packed_rows(tok, width)
    mean = jnp.sum(lat, axis=0, keepdims=True) / float(tok)
    hi = mean.astype(jnp.bfloat16).astype(jnp.float32)
    lo = (mean - hi).astype(jnp.bfloat16).astype(jnp.float32)
    diff = lat - (hi + lo)
    cuts = [slice(at, at + LANES) for at in range(0, width, LANES)]
    for n, cut in enumerate(cuts):
        out[n * tok : (n + 1) * tok, :] = diff[:, cut].astype(jnp.bfloat16)
    rows = [hi[:, cut] for cut in cuts] + [lo[:, cut] for cut in cuts]
    if len(rows) < mean_rows:
        rows.append(jnp.zeros((mean_rows - len(rows), LANES), jnp.float32))
    out[body_rows:, :] = jnp.concatenate(rows, axis=0).astype(jnp.bfloat16)


def unpack_latent(packed, target, start, tok):
    width = target.shape[1]
    body_rows, _ = packed_rows(tok, width)
    chunks = width // LANES
    means = packed[body_rows:, :].astype(jnp.float32)
    for n in range(chunks):
        mean = means[n : n + 1] + means[chunks + n : chunks + n + 1]
        diff = packed[n * tok : (n + 1) * tok, :].astype(jnp.float32)
        target[start : start + tok, n * LANES : (n + 1) * LANES] = diff + mean


def prepare_kernel(images, refs):
    keys, values, text_k, text_v, lat, kv_out, txt_out, lat_out = refs
    c = lax.axis_index("cfg")
    pack_latent(lat[0], lat_out)
    for i in range(images):
        kv_out[0, i] = keys[c * images + i]
        kv_out[1, i] = values[c * images + i]
    ctx, width = text_k.shape[1:]
    pad = jnp.zeros((txt_out.shape[1] - ctx, width), jnp.float32)
    for n, ref in enumerate((text_k, text_v)):
        rows = jnp.concatenate([ref[0].astype(jnp.float32), pad], axis=0)
        txt_out[n] = rows.astype(jnp.bfloat16)


def guidance():
    first = lax.axis_index("cfg") == 0
    return (
        jnp.where(first, guide_weight, 1.0 - guide_weight),
        jnp.where(first, 1.0 - guide_weight, guide_weight),
    )


def is_keeper(images):
    mine = lax.axis_index("batch") // images if images > 1 else lax.axis_index("batch")
    return mine == lax.axis_index("cfg")


def project(normed, weight):
    return jnp.dot(normed, weight[...], preferred_element_type=jnp.float32).astype(jnp.bfloat16)


def first_project(images, patches, refs):
    (t_ref, wq, wk, wv, gain, bias, lat_here) = refs[:7]
    n = 7
    lats = refs[n : n + images * patches]
    state_s, q_out, k_out, v_out, samp, member, member_t = refs[n + images * patches :]
    tok, width = lat_here.shape[1:]
    member[...], member_t[...] = group_matrices(width)
    bars = alpha_bars(t_ref)
    for k in range(STEPS):
        for n_row, value in enumerate(sampler_weights(bars, k)):
            at = 2 * k + n_row
            samp[at : at + 1, :] = jnp.broadcast_to(value, (1, LANES))
    keeper = is_keeper(images)
    for i in range(images):
        own = lats[i * patches][...]
        if images == 1:
            own = jnp.where(keeper, lat_here[0], own)
        state_s[i, 0:tok, :] = own
        for k in range(1, patches):
            unpack_latent(lats[i * patches + k], state_s.at[i], k * tok, tok)
        state = state_s[i]
        mean, factor = norm_factors(
            state, gain[...].reshape(1, -1), member[...], member_t[...]
        )
        normed = ((state - mean) * factor + bias[...].reshape(1, -1)).astype(jnp.bfloat16)
        q_out[i] = project(normed, wq)
        k_out[i] = project(normed, wk)
        v_out[i] = project(normed, wv)


def first_attend(images, patches, ctx, refs):
    (samp, wo, txt_a, txt_b, kv_own, state, q, k_new, v_new) = refs[:9]
    n = 9
    kvs = refs[n : n + patches - 1]
    base, send, key_s, val_s, att_s = refs[n + patches - 1 :]
    rows = state.shape[1]
    tok = rows // patches
    keep = samp[0:1, 0:1]
    push = samp[1:2, 0:1]
    guides = guidance()
    texts = ((txt_a.at[0], txt_a.at[1]), (txt_b.at[0], txt_b.at[1]))
    for i in range(images):
        key_s[rows : 2 * rows, :] = k_new[i]
        val_s[rows : 2 * rows, :] = v_new[i]
        key_s[0:tok, :] = kv_own[0, i]
        val_s[0:tok, :] = kv_own[1, i]
        for k in range(1, patches):
            key_s[k * tok : (k + 1) * tok, :] = kvs[k - 1][0, i]
            val_s[k * tok : (k + 1) * tok, :] = kvs[k - 1][1, i]

        def block(start, size):
            row = lax.broadcasted_iota(jnp.int32, (size, 2 * rows), 0) + start
            col = lax.broadcasted_iota(jnp.int32, (size, 2 * rows), 1)
            fresh_col = col >= rows
            same = block_of(row, tok) == block_of(jnp.where(fresh_col, col - rows, col), tok)
            mask = same == fresh_col
            pieces = attend(
                q[i, pl.ds(start, size), :], key_s, val_s, texts, ctx, guides, mask
            )
            for n_piece, piece in enumerate(pieces):
                at = n_piece * LANES
                att_s[pl.ds(start, size), at : at + piece.shape[1]] = piece

        size = min(rows, ROW_BLOCK)
        if rows % size:
            size = tok
        if rows == size:
            block(0, rows)
        else:

            def step(j, carry):
                block(pl.multiple_of(j * size, size), size)
                return carry

            lax.fori_loop(0, rows // size, step, 0)
        part = push * jnp.dot(att_s[...], wo[...], preferred_element_type=jnp.float32)
        send[i] = part.astype(jnp.bfloat16)
        base[i] = (keep + push) * state[i] + part


def last_project(images, patches, peers, refs):
    (wq, wk, wv, gain, bias, member, member_t, base) = refs[:8]
    others = refs[8 : 8 + peers]
    own_out, q_out, kv_out, state_s = refs[8 + peers :]
    rows = state_s.shape[0]
    tok = rows // patches
    for i in range(images):
        state = base[i]
        for other in others:
            state = state + other[i].astype(jnp.float32)
        state_s[...] = state
        mean, factor = norm_factors(
            state_s[...], gain[...].reshape(1, -1), member[...], member_t[...]
        )
        own = state_s[0:tok, :]
        own_out[i] = own
        normed = ((own - mean) * factor + bias[...].reshape(1, -1)).astype(jnp.bfloat16)
        q_out[i] = project(normed, wq)
        kv_out[0, i] = project(normed, wk)
        kv_out[1, i] = project(normed, wv)


def last_attend(images, ctx, refs):
    (samp, wo, txt_a, txt_b, own, q, kv_new, k_old, v_old) = refs[:9]
    base_out, part_out, ring_out, key_s, val_s = refs[9:]
    rows = key_s.shape[0]
    tok = own.shape[1]
    keep = samp[2:3, 0:1]
    push = samp[3:4, 0:1]
    guides = guidance()
    texts = ((txt_a.at[0], txt_a.at[1]), (txt_b.at[0], txt_b.at[1]))
    for i in range(images):
        key_s[0:tok, :] = kv_new[0, i]
        val_s[0:tok, :] = kv_new[1, i]
        key_s[tok:rows, :] = k_old[i, tok:rows, :]
        val_s[tok:rows, :] = v_old[i, tok:rows, :]
        pieces = attend(q[i], key_s, val_s, texts, ctx, guides, None)
        att = jnp.concatenate(pieces, axis=1)
        part = push * jnp.dot(att, wo[...], preferred_element_type=jnp.float32)
        part_out[i] = part
        kept = (keep + push) * own[i] + part
        base_out[i] = kept
        ring_out[i] = jnp.where(is_keeper(images), kept, part)


def end_kernel(images, extra, refs):
    base, ring, diag, kv, kv_far = refs[:5]
    others = refs[5 : 5 + 2 * extra]
    latent, keys, values = refs[5 + 2 * extra :]
    keeper = is_keeper(images)
    total = ring[...] + jnp.where(keeper, base[...], diag[...])
    for r in range(extra):
        total = total + jnp.where(keeper, others[2 * r][...], others[2 * r + 1][...])
    latent[0] = total
    c = lax.axis_index("cfg")
    for i in range(images):
        keys[c * images + i] = kv[0, i]
        values[c * images + i] = kv[1, i]
        keys[(1 - c) * images + i] = kv_far[0, i]
        values[(1 - c) * images + i] = kv_far[1, i]


def kernel_call(body, args, outs, scratch, scalars=0, final=False, cost=None):
    def run(*refs):
        body(refs)

    return pl.pallas_call(
        run,
        out_shape=[
            jax.ShapeDtypeStruct(s, d) if final else pltpu.VMEM(s, d) for s, d in outs
        ],
        in_specs=[SMEM] * scalars + [VMEM] * (len(args) - scalars),
        out_specs=[VMEM] * len(outs),
        scratch_shapes=[pltpu.VMEM(s, d) for s, d in scratch],
        compiler_params=pltpu.CompilerParams(vmem_limit_bytes=VMEM_LIMIT),
        cost_estimate=cost,
    )(*args)


class Grid:
    def __init__(self, mesh):
        self.axes = ("patch", "cfg", "batch")
        self.sizes = tuple(mesh.shape[a] for a in self.axes)

    def flat(self, p, c, b):
        return (p * self.sizes[1] + c) * self.sizes[2] + b

    def pull(self, x, source):
        pairs = []
        for p in range(self.sizes[0]):
            for c in range(self.sizes[1]):
                for b in range(self.sizes[2]):
                    src = source(p, c, b)
                    if src is not None and src != (p, c, b):
                        pairs.append((self.flat(*src), self.flat(p, c, b)))
        return lax.ppermute(x, self.axes, pairs)


def pick(stack, index):
    if len(stack) == 1:
        return stack[0]
    return lax.dynamic_index_in_dim(jnp.stack(stack), index, 0, keepdims=False)


def body(
    grid,
    latent,
    stale_keys,
    stale_values,
    text_keys,
    text_values,
    w_query,
    w_key,
    w_value,
    w_out,
    norm_gain,
    norm_bias,
    timesteps,
):
    patches, halves, batch = grid.sizes
    state = latent[0]
    tok, width = state.shape
    images = stale_keys.shape[0]
    mine = images // halves
    local = w_query.shape[1]
    ctx = text_keys.shape[1]
    ctx_pad = -(-ctx // 16) * 16
    rows = tok * patches
    b = lax.axis_index("batch")

    def away(p, s):
        return p ^ s if patches & (patches - 1) == 0 else (p - s) % patches

    def other_core(p, cc, bb):
        return (p, 1 - cc, bb)

    def latent_source(k, s):
        def source(p, cc, bb):
            if mine == 1 and s == 0:
                return (p, 1 - cc, 1 - bb)
            x = cc * mine + (bb + k) % mine
            return (away(p, s), cc if bb // mine == cc else 1 - cc, x)

        return source

    kv_own, txt_own, lat_own = kernel_call(
        functools.partial(prepare_kernel, mine),
        [stay(x) for x in (stale_keys, stale_values, text_keys, text_values, latent)],
        [
            ((2, mine, tok, local), jnp.bfloat16),
            ((2, ctx_pad, local), jnp.bfloat16),
            ((sum(packed_rows(tok, width)), LANES), jnp.bfloat16),
        ],
        [],
        cost=LONG,
    )
    slots = [
        [grid.pull(lat_own if s else state, latent_source(k, s)) for s in range(patches)]
        for k in range(mine)
    ]
    if mine > 1:
        slots[0][0] = jnp.where(is_keeper(mine), state, slots[0][0])
    lat = [
        pick([slots[k][s] for k in range(mine)], (i - b) % mine)
        for i in range(mine)
        for s in range(patches)
    ]
    kvs = [
        grid.pull(kv_own, lambda p, cc, bb, s=s: (away(p, s), cc, bb)) for s in range(1, patches)
    ]
    txt_far = grid.pull(txt_own, other_core)

    qkv = [near(w) for w in (w_query, w_key, w_value)]
    out_weight = near(w_out)
    affine = [stay(norm_gain), stay(norm_bias)]
    texts = [near(txt_own), near(txt_far)]
    full = ((mine, rows, local), jnp.bfloat16)
    state0, q0, k0, v0, samp, *member = kernel_call(
        functools.partial(first_project, mine, patches),
        [stay(timesteps)] + qkv + affine + [stay(latent)] + [near(x) for x in lat],
        [
            ((mine, rows, width), jnp.float32),
            full,
            full,
            full,
            ((2 * STEPS, LANES), jnp.float32),
            ((width, LANES), jnp.bfloat16),
            ((LANES, width), jnp.bfloat16),
        ],
        [],
        scalars=1,
    )
    base, send = kernel_call(
        functools.partial(first_attend, mine, patches, ctx),
        [near(samp), out_weight]
        + texts
        + [near(x) for x in [kv_own, state0, q0, k0, v0] + kvs],
        [((mine, rows, width), jnp.float32), ((mine, rows, width), jnp.bfloat16)],
        [
            ((2 * rows, local), jnp.bfloat16),
            ((2 * rows, local), jnp.bfloat16),
            ((rows, local), jnp.bfloat16),
        ],
    )
    others = [
        grid.pull(send, lambda p, cc, bb, r=r: (p, cc, (bb + r) % batch)) for r in range(1, batch)
    ]
    own1, q1, kv1 = kernel_call(
        functools.partial(last_project, mine, patches, batch - 1),
        qkv + affine + [near(x) for x in member + [base] + others],
        [
            ((mine, tok, width), jnp.float32),
            ((mine, tok, local), jnp.bfloat16),
            ((2, mine, tok, local), jnp.bfloat16),
        ],
        [((rows, width), jnp.float32)],
    )
    kv_far = grid.pull(kv1, other_core)
    base1, part1, ring1 = kernel_call(
        functools.partial(last_attend, mine, ctx),
        [near(samp), out_weight] + texts + [near(x) for x in [own1, q1, kv1, k0, v0]],
        [((mine, tok, width), jnp.float32)] * 3,
        [((rows, local), jnp.bfloat16), ((rows, local), jnp.bfloat16)],
        cost=LONG,
    )

    own_base = pick([base1[i] for i in range(mine)], b % mine)
    ends = []
    for r in [mine] + [r for r in range(1, batch) if r != mine]:
        part = pick([part1[i] for i in range(mine)], ((b - r) % batch) % mine)

        def to_keeper(p, cc, bb, r=r):
            if bb // mine == cc:
                return (p, cc, (bb + r) % batch)
            return (p, 1 - cc, bb) if r == mine else None

        def to_partner(p, cc, bb, r=r):
            if mine == 1:
                return (p, 1 - cc, 1 - bb)
            return None if bb // mine == cc else (p, 1 - cc, (bb + r) % batch)

        sent = part
        if r == mine:
            sent = ring1[0] if mine == 1 else jnp.where(is_keeper(mine), own_base, part)
        ends.append(grid.pull(sent, to_keeper))
        ends.append(grid.pull(part, to_partner))
    final = kernel_call(
        functools.partial(end_kernel, mine, batch - 2),
        [near(x) for x in [own_base, ends[0], ends[1], kv1, kv_far] + ends[2:]],
        [
            ((1, tok, width), jnp.float32),
            ((images, tok, local), jnp.bfloat16),
            ((images, tok, local), jnp.bfloat16),
        ],
        [],
        final=True,
    )
    return tuple(final)


def solution(mesh):
    return jax.shard_map(
        functools.partial(body, Grid(mesh)),
        mesh=mesh,
        in_specs=(
            P(("prompts", "batch"), "patch", None),
            P("prompts", "patch", "batch"),
            P("prompts", "patch", "batch"),
            P(("prompts", "cfg"), None, "batch"),
            P(("prompts", "cfg"), None, "batch"),
            P(None, "batch"),
            P(None, "batch"),
            P(None, "batch"),
            P("batch", None),
            P(),
            P(),
            P("prompts"),
        ),
        out_specs=(
            P(("prompts", "batch"), "patch", None),
            P("prompts", "patch", "batch"),
            P("prompts", "patch", "batch"),
        ),
        check_vma=False,
    )
```
